512 devices in a mesh: rows: 64 (over z, y), cols: 8 (over x, core).
Axes of the slice: x: 4, y: 8, z: 8, core: 2. Of those that a mesh axis runs over, the one named last changes fastest.
Arguments:
- basis_values: bfloat16 [8192, 512, 128], P(('rows', 'cols')), may hold values from -0.125 to 0.125
- potential: float32 [262144], P(('rows', 'cols')), may hold values from -6 to 6
- contrib_index: int32 [65536, 4], P(('rows', 'cols')), may hold values from 0 to 63, as said below
- pattern: int32 [64, 128, 2], P('rows'), may hold values from 0 to 135, as said below
- ghost_list: int32 [64, 64, 2], P('rows'), may hold values from -1 to 511, as said below
- state: float32 [512, 65536], P('cols', 'rows'), may hold values from -6 to 6
- damp_lower: float32 [1], replicated, may hold values from -2.5 to -1
- damp_upper: float32 [1], replicated, may hold values from 1 to 2.5
Outputs:
- first_term: float32 [512, 65536], P('cols', 'rows')
- second_term: float32 [512, 65536], P('cols', 'rows')
The draws below stay inside these ranges and needn't reach their ends.
Inputs may be any that keep to these rules, and one draw needn't show every extreme that they name: `contrib_index`: column 0 is the rows index that receives the contribution, column 1 its slot among the 16 slots held by the device of that rows index with the sender's cols index, columns 2 and 3 blocks of the sender's batch (below 16). Among the 128 rows of one device at most 4 name the same rows index, and those that do all name the same slot; one rows index receives 4 from every device. pattern[q, g, 0] is below 8. pattern[q, g, 1] is below 8 exactly for the first 4 of each 16 slots; above that it points at an entry of ghost_list[q] that is not -1, and every such entry is pointed at by some slot. ghost_list[q, p, :] holds distinct row blocks owned by rows index p (from p * 8 to p * 8 + 7) or -1; always -1 where p equals q; exactly 48 entries of ghost_list[q] are not -1, and for each q some p has 2 of them.
All inputs are finite; a program needn't handle non-finite values.
Results may differ from the reference program's by a relative error of at most 0.0079.
Values may be sent and summed in bfloat16 or wider, within the bound.
No kernel may reach another device: no remote copies, remote signals or barrier semaphores. Data moves between devices by JAX's collectives and lax.ppermute only.
A program may use at most 64 MiB of HBM per device.

```python
import jax
import jax.numpy as jnp
from jax import lax

BS = 128
NVEC = 512
RB_DEV = 8
NG = 512
LB = 16
CAP = 4
GCAP = 2
NB = 512
NORB = 65536
K_GRP = 128
K_DEV = 16
K_IN = 4
CONTRIB = 128
NGHOST = 48
N_ROWS = 64
N_COLS = 8
DEVICES = 512


def ghost_choice(key):
    base_key = jax.random.fold_in(key, 21)
    local_scores = jax.random.randint(jax.random.fold_in(base_key, 1), (N_ROWS, N_ROWS, RB_DEV), 0, 4096) * RB_DEV + jnp.arange(RB_DEV, dtype=jnp.int32)
    local_order = jnp.argsort(local_scores, axis=-1)[:, :, :GCAP].astype(jnp.int32)
    owner_ids = jnp.arange(N_ROWS, dtype=jnp.int32)
    global_ids = owner_ids[None, :, None] * RB_DEV + local_order
    positions = jnp.arange(N_ROWS * GCAP, dtype=jnp.int32)
    position_owner = positions // GCAP
    favored = (owner_ids + 1 + jax.random.randint(jax.random.fold_in(base_key, 2), (N_ROWS,), 0, N_ROWS - 1)) % N_ROWS
    priority = jax.random.randint(jax.random.fold_in(base_key, 3), (N_ROWS, N_ROWS * GCAP), 0, 4096)
    priority = jnp.where(position_owner[None, :] == favored[:, None], 4096, priority)
    priority = jnp.where(position_owner[None, :] == owner_ids[:, None], -1, priority)
    ranked = priority * (N_ROWS * GCAP) + positions[None, :]
    chosen = jnp.argsort(-ranked, axis=-1)[:, :NGHOST].astype(jnp.int32)
    listed = jnp.any(positions[None, None, :] == chosen[:, :, None], axis=1)
    table = jnp.where(listed.reshape(N_ROWS, N_ROWS, GCAP), global_ids, -1).astype(jnp.int32)
    return (table, chosen)


def draw_ghost_list(key, part):
    return ghost_choice(key)[0]


def draw_pattern(key, part):
    table, chosen = ghost_choice(key)
    base_key = jax.random.fold_in(key, 22)
    outer_count = K_DEV - K_IN
    ghost_slots = N_COLS * outer_count
    shuffle_scores = jax.random.randint(jax.random.fold_in(base_key, 1), (N_ROWS, ghost_slots), 0, 4096) * ghost_slots + jnp.arange(ghost_slots, dtype=jnp.int32)
    shuffled = jnp.argsort(shuffle_scores, axis=-1).astype(jnp.int32)
    entries = jnp.take_along_axis(chosen, shuffled % NGHOST, axis=1)
    outer_src = (RB_DEV + entries).reshape(N_ROWS, N_COLS, outer_count)
    inner_src = jax.random.randint(jax.random.fold_in(base_key, 2), (N_ROWS, N_COLS, K_IN), 0, RB_DEV)
    sources = jnp.concatenate([inner_src, outer_src], axis=2).reshape(N_ROWS, K_GRP)
    row_ids = jax.random.randint(jax.random.fold_in(base_key, 3), (N_ROWS, K_GRP), 0, RB_DEV)
    return jnp.stack([row_ids, sources], axis=-1).astype(jnp.int32)


def draw_contrib_index(key, part):
    base_key = jax.random.fold_in(key, 23)
    row_ids = jnp.arange(N_ROWS, dtype=jnp.int32)
    hotness = jax.random.randint(jax.random.fold_in(base_key, 1), (N_ROWS,), 0, 3)
    hottest = jax.random.randint(jax.random.fold_in(base_key, 2), (), 0, N_ROWS)
    hotness = jnp.where(row_ids == hottest, 3, hotness)

    def one_device(device):
        device_key = jax.random.fold_in(base_key, 100 + device)
        slot_ids = jnp.arange(N_ROWS * CAP, dtype=jnp.int32)
        noise = jax.random.randint(jax.random.fold_in(device_key, 1), (N_ROWS * CAP,), 0, 4096)
        scores = (hotness[slot_ids // CAP] * 4096 + noise) * 1024 + slot_ids
        picked = jnp.argsort(-scores)[:CONTRIB].astype(jnp.int32)
        mixing = jax.random.randint(jax.random.fold_in(device_key, 2), (CONTRIB,), 0, 4096) * CONTRIB + jnp.arange(CONTRIB, dtype=jnp.int32)
        picked = picked[jnp.argsort(mixing)]
        target_row = picked // CAP
        slot_table = jax.random.randint(jax.random.fold_in(device_key, 3), (N_ROWS,), 0, K_DEV)
        target_slot = slot_table[target_row]
        block_pair = jax.random.randint(jax.random.fold_in(device_key, 4), (CONTRIB, 2), 0, LB)
        return jnp.concatenate([target_row[:, None], target_slot[:, None], block_pair], axis=1)
    result = jax.vmap(one_device)(jnp.arange(DEVICES, dtype=jnp.int32))
    return result.reshape(DEVICES * CONTRIB, 4).astype(jnp.int32)


def shard_levels(key, shape, split, low, largest):
    loudness, own = 1.0, jax.random.fold_in(key, 6)
    for axis_at, blocks in split:
        steps = jnp.exp(jax.random.uniform(jax.random.fold_in(own, axis_at), (blocks,), jnp.float32, low / len(split), largest / len(split)))
        loudness = loudness * jnp.repeat(steps, shape[axis_at] // blocks).reshape([-1 if axis == axis_at else 1 for axis in range(len(shape))])
    return loudness


def scatter_about(key, extent, scale, limit, shards=(), kind=jnp.bfloat16):
    factor_of = shard_levels(key, extent, shards, -0.22, 0.18) if shards else 1.0
    values = jax.random.normal(key, extent, jnp.float32) * scale * factor_of
    return jnp.minimum(jnp.maximum(values, -limit), limit).astype(kind)


def setup_inputs(seed: int = 0) -> dict:
    keys = jax.random.split(jax.random.key(seed), 9)
    basis_values = scatter_about(keys[0], (N_ROWS * N_COLS * LB, NG, BS), (4 * NG) ** -0.5, 0.125, ((0, 512),))
    potential = scatter_about(keys[1], (N_ROWS * N_COLS * NG,), 1.0, 6.0, ((0, 512),), jnp.float32)
    contrib_index = draw_contrib_index(jax.random.fold_in(keys[8], 71), 0)
    pattern = draw_pattern(jax.random.fold_in(keys[8], 71), 0)
    ghost_list = draw_ghost_list(jax.random.fold_in(keys[8], 71), 0)
    state = scatter_about(keys[5], (NVEC, NORB), 1.0, 6.0, ((0, 8), (1, 64)), jnp.float32)
    damp_lower = jnp.clip(jax.random.uniform(keys[6], (1,), jnp.float32, -2.5, -1.0), -2.5, -1.0)
    damp_upper = jnp.clip(jax.random.uniform(keys[7], (1,), jnp.float32, 1.0, 2.5), 1.0, 2.5)
    return dict(basis_values=basis_values, potential=potential, contrib_index=contrib_index, pattern=pattern, ghost_list=ghost_list, state=state, damp_lower=damp_lower, damp_upper=damp_upper)


def reference(basis_values, potential, contrib_index, pattern, ghost_list, state, damp_lower, damp_upper):
    device_count = N_ROWS * N_COLS
    basis = basis_values.reshape(device_count, LB, NG, BS)
    grid_weights = potential.reshape(device_count, NG)
    contribs = contrib_index.reshape(device_count, CONTRIB, 4)
    column_ids = jnp.arange(device_count, dtype=jnp.int32) % N_COLS

    def add_device(summed, item):
        values, weights, indices, column = item
        weighted = (values.astype(jnp.float32) * weights[None, :, None]).astype(jnp.bfloat16)
        left_vals = values[indices[:, 2]].astype(jnp.float32)
        right_vals = weighted[indices[:, 3]].astype(jnp.float32)
        tile_set = jnp.einsum("snx,sny->sxy", left_vals, right_vals).astype(jnp.bfloat16)
        slot_ids = (column * K_DEV + indices[:, 1]).astype(jnp.int32)
        summed = summed.at[indices[:, 0], slot_ids].add(tile_set.astype(jnp.float32))
        return summed, None

    empty_sum = jnp.zeros((N_ROWS, K_GRP, BS, BS), jnp.float32)
    summed, unused = lax.scan(add_device, empty_sum, (basis, grid_weights, contribs, column_ids))
    hamiltonian = summed.astype(jnp.bfloat16)

    group_ids = jnp.arange(N_ROWS, dtype=jnp.int32)
    local_src = pattern[:, :, 1]
    flat_ghosts = ghost_list.reshape(N_ROWS, N_ROWS * GCAP)
    ghost_pick = jnp.take_along_axis(flat_ghosts, jnp.clip(local_src - RB_DEV, 0, N_ROWS * GCAP - 1), axis=1)
    col_ids = jnp.where(local_src < RB_DEV, group_ids[:, None] * RB_DEV + local_src, ghost_pick).astype(jnp.int32)
    row_ids = pattern[:, :, 0]

    lower_end = damp_lower[0]
    upper_end = damp_upper[0]
    center = (upper_end + lower_end) / 2.0
    half_width = (upper_end - lower_end) / 2.0

    def apply_hamiltonian(vectors):
        blocks = vectors.astype(jnp.bfloat16).reshape(NVEC, NB, BS)

        def group_rows(owner):
            operands = jnp.take(blocks, col_ids[owner], axis=1).astype(jnp.float32)
            products = jnp.einsum("vkb,kab->vka", operands, hamiltonian[owner].astype(jnp.float32))
            onehot = (row_ids[owner][:, None] == jnp.arange(RB_DEV, dtype=jnp.int32)[None, :]).astype(jnp.float32)
            return jnp.einsum("vka,ki->via", products, onehot, precision=lax.Precision.HIGHEST)

        result = lax.map(group_rows, group_ids)
        return result.transpose(1, 0, 2, 3).reshape(NVEC, NORB)

    first_term = (apply_hamiltonian(state) - center * state) / half_width
    second_term = 2.0 * (apply_hamiltonian(first_term) - center * first_term) / half_width - state
    return first_term, second_term
```

```python
import jax
import jax.numpy as jnp
from jax import lax
from jax.sharding import PartitionSpec as P


def on_device(
    basis_values, potential, contrib_index, pattern, ghost_list, state, damp_lower, damp_upper
):
    n_rows = lax.axis_size("rows")
    n_cols = lax.axis_size("cols")
    basis_blocks, points, block_size = basis_values.shape
    vec_count = state.shape[0]
    row_blocks = state.shape[1] // block_size
    group_slots = pattern.shape[1]
    slot_count = group_slots // n_cols
    ghost_width = ghost_list.shape[2]
    pair_count = basis_blocks * basis_blocks

    ghost_ids = ghost_list[0]
    owners = jnp.arange(n_rows, dtype=jnp.int32)[:, None] * row_blocks
    requested = jnp.where(ghost_ids >= 0, ghost_ids - owners, -1)
    target_row = contrib_index[:, 0]
    to_target = target_row[:, None] == jnp.arange(n_rows, dtype=jnp.int32)[None, :]
    slot_for_target = jnp.max(jnp.where(to_target, contrib_index[:, 1:2], -1), axis=0)
    index_send = jnp.concatenate([requested, slot_for_target[:, None]], axis=1)
    index_recv = lax.all_to_all(index_send, "rows", split_axis=0, concat_axis=0, tiled=True)
    wanted_by = index_recv[:, :ghost_width]
    arrived_slots = index_recv[:, ghost_width]

    center = (damp_upper[0] + damp_lower[0]) / 2.0
    half_width = (damp_upper[0] - damp_lower[0]) / 2.0

    def own_blocks(vectors):
        return (
            vectors.astype(jnp.bfloat16)
            .reshape(vec_count, row_blocks, block_size)
            .transpose(1, 0, 2)
        )

    def with_ghosts(blocks):
        outgoing = jnp.where(
            (wanted_by >= 0)[:, :, None, None],
            blocks[jnp.clip(wanted_by, 0, row_blocks - 1)],
            jnp.zeros((), jnp.bfloat16),
        )
        arrived = lax.all_to_all(outgoing, "rows", split_axis=0, concat_axis=0, tiled=True)
        return jnp.concatenate(
            [blocks, arrived.reshape(n_rows * ghost_width, vec_count, block_size)], axis=0
        )

    state_blocks = own_blocks(state)
    state_pool = with_ghosts(state_blocks)

    weighted = (basis_values.astype(jnp.float32) * potential[None, :, None]).astype(jnp.bfloat16)
    pair_tiles = jnp.einsum(
        "anx,bny->abxy", basis_values, weighted, preferred_element_type=jnp.float32
    ).astype(jnp.bfloat16)
    pair_id = contrib_index[:, 2] * basis_blocks + contrib_index[:, 3]
    pair_hot = (pair_id[:, None] == jnp.arange(pair_count, dtype=jnp.int32)[None, :]).astype(
        jnp.bfloat16
    )
    counts = jnp.dot(
        to_target.astype(jnp.bfloat16).T, pair_hot, preferred_element_type=jnp.float32
    ).astype(jnp.bfloat16)
    send_tiles = jnp.dot(
        counts,
        pair_tiles.reshape(pair_count, block_size * block_size),
        preferred_element_type=jnp.float32,
    ).astype(jnp.bfloat16).reshape(n_rows, block_size, block_size)
    arrived_tiles = lax.all_to_all(send_tiles, "rows", split_axis=0, concat_axis=0, tiled=True)
    slot_wanted = jnp.arange(slot_count, dtype=jnp.int32)
    selector = (arrived_slots[None, :] == slot_wanted[:, None]).astype(jnp.bfloat16)
    assembled = jnp.dot(
        selector,
        arrived_tiles.reshape(n_rows, block_size * block_size),
        preferred_element_type=jnp.float32,
    )
    assembled = assembled.astype(jnp.bfloat16).reshape(slot_count, block_size, block_size)
    group_tiles = lax.all_gather(assembled, "cols", axis=0, tiled=True)

    rows_local = pattern[0, :, 0]
    sources = pattern[0, :, 1]

    def accumulate(tile_part, source_part, row_part, operand_pool):
        operands = operand_pool[source_part]
        products = jnp.einsum(
            "kvb,kab->kva", operands, tile_part, preferred_element_type=jnp.float32
        )
        row_select = (row_part[:, None] == jnp.arange(row_blocks, dtype=jnp.int32)[None, :]).astype(
            jnp.float32
        )
        return jnp.einsum("ki,kva->iva", row_select, products, precision=lax.Precision.HIGHEST)

    def as_field(running):
        return running.transpose(1, 0, 2).reshape(vec_count, row_blocks * block_size)

    first_image = as_field(accumulate(group_tiles, sources, rows_local, state_pool))
    first_term = (first_image - center * state) / half_width
    first_pool = with_ghosts(own_blocks(first_term))
    second_image = as_field(accumulate(group_tiles, sources, rows_local, first_pool))
    second_term = 2.0 * (second_image - center * first_term) / half_width - state
    return (first_term, second_term)


def solution(mesh):
    in_specs = (
        P(("rows", "cols"), None, None),
        P(("rows", "cols")),
        P(("rows", "cols"), None),
        P("rows", None, None),
        P("rows", None, None),
        P("cols", "rows"),
        P(),
        P(),
    )
    out_specs = (P("cols", "rows"), P("cols", "rows"))
    return jax.shard_map(
        on_device, mesh=mesh, in_specs=in_specs, out_specs=out_specs, check_vma=False
    )
```

```python
import jax
import jax.numpy as jnp
from jax import lax
from jax.sharding import PartitionSpec as P


def on_device(
    basis_values, potential, contrib_index, pattern, ghost_list, state, damp_lower, damp_upper
):
    n_rows = lax.axis_size("rows")
    n_cols = lax.axis_size("cols")
    basis_blocks, points, block_size = basis_values.shape
    vec_count = state.shape[0]
    row_blocks = state.shape[1] // block_size
    group_slots = pattern.shape[1]
    slot_count = group_slots // n_cols
    ghost_width = ghost_list.shape[2]
    pair_count = basis_blocks * basis_blocks

    ghost_ids = ghost_list[0]
    owners = jnp.arange(n_rows, dtype=jnp.int32)[:, None] * row_blocks
    requested = jnp.where(ghost_ids >= 0, ghost_ids - owners, -1)
    target_row = contrib_index[:, 0]
    to_target = target_row[:, None] == jnp.arange(n_rows, dtype=jnp.int32)[None, :]
    slot_for_target = jnp.max(jnp.where(to_target, contrib_index[:, 1:2], -1), axis=0)
    index_send = jnp.concatenate([requested, slot_for_target[:, None]], axis=1)
    index_recv = lax.all_to_all(index_send, "rows", split_axis=0, concat_axis=0, tiled=True)
    wanted_by = index_recv[:, :ghost_width]
    arrived_slots = index_recv[:, ghost_width]

    center = (damp_upper[0] + damp_lower[0]) / 2.0
    half_width = (damp_upper[0] - damp_lower[0]) / 2.0

    def own_blocks(vectors):
        return (
            vectors.astype(jnp.bfloat16)
            .reshape(vec_count, row_blocks, block_size)
            .transpose(1, 0, 2)
        )

    def with_ghosts(blocks):
        outgoing = jnp.where(
            (wanted_by >= 0)[:, :, None, None],
            blocks[jnp.clip(wanted_by, 0, row_blocks - 1)],
            jnp.zeros((), jnp.bfloat16),
        )
        arrived = lax.all_to_all(outgoing, "rows", split_axis=0, concat_axis=0, tiled=True)
        return jnp.concatenate(
            [blocks, arrived.reshape(n_rows * ghost_width, vec_count, block_size)], axis=0
        )

    state_blocks = own_blocks(state)
    state_pool = with_ghosts(state_blocks)

    weighted = (basis_values.astype(jnp.float32) * potential[None, :, None]).astype(jnp.bfloat16)
    pair_tiles = jnp.einsum(
        "anx,bny->abxy", basis_values, weighted, preferred_element_type=jnp.float32
    ).astype(jnp.bfloat16)
    pair_id = contrib_index[:, 2] * basis_blocks + contrib_index[:, 3]
    pair_hot = (pair_id[:, None] == jnp.arange(pair_count, dtype=jnp.int32)[None, :]).astype(
        jnp.bfloat16
    )
    counts = jnp.dot(
        to_target.astype(jnp.bfloat16).T, pair_hot, preferred_element_type=jnp.float32
    ).astype(jnp.bfloat16)
    send_tiles = jnp.dot(
        counts,
        pair_tiles.reshape(pair_count, block_size * block_size),
        preferred_element_type=jnp.float32,
    ).astype(jnp.bfloat16).reshape(n_rows, block_size, block_size)
    send_tiles, state_pool = lax.optimization_barrier((send_tiles, state_pool))
    arrived_tiles = lax.all_to_all(send_tiles, "rows", split_axis=0, concat_axis=0, tiled=True)
    slot_wanted = jnp.arange(slot_count, dtype=jnp.int32)
    selector = (arrived_slots[None, :] == slot_wanted[:, None]).astype(jnp.bfloat16)
    assembled = jnp.dot(
        selector,
        arrived_tiles.reshape(n_rows, block_size * block_size),
        preferred_element_type=jnp.float32,
    )
    assembled = assembled.astype(jnp.bfloat16).reshape(slot_count, block_size, block_size)
    group_tiles = lax.all_gather(assembled, "cols", axis=0, tiled=True)

    rows_local = pattern[0, :, 0]
    sources = pattern[0, :, 1]

    def accumulate(tile_part, source_part, row_part, operand_pool):
        operands = operand_pool[source_part]
        products = jnp.einsum(
            "kvb,kab->kva", operands, tile_part, preferred_element_type=jnp.float32
        )
        row_select = (row_part[:, None] == jnp.arange(row_blocks, dtype=jnp.int32)[None, :]).astype(
            jnp.float32
        )
        return jnp.einsum("ki,kva->iva", row_select, products, precision=lax.Precision.HIGHEST)

    def as_field(running):
        return running.transpose(1, 0, 2).reshape(vec_count, row_blocks * block_size)

    first_image = as_field(accumulate(group_tiles, sources, rows_local, state_pool))
    first_term = (first_image - center * state) / half_width
    first_pool = with_ghosts(own_blocks(first_term))
    second_image = as_field(accumulate(group_tiles, sources, rows_local, first_pool))
    second_term = 2.0 * (second_image - center * first_term) / half_width - state
    return (first_term, second_term)


def solution(mesh):
    in_specs = (
        P(("rows", "cols"), None, None),
        P(("rows", "cols")),
        P(("rows", "cols"), None),
        P("rows", None, None),
        P("rows", None, None),
        P("cols", "rows"),
        P(),
        P(),
    )
    out_specs = (P("cols", "rows"), P("cols", "rows"))
    return jax.shard_map(
        on_device, mesh=mesh, in_specs=in_specs, out_specs=out_specs, check_vma=False
    )
```

```python
import jax
import jax.numpy as jnp
from jax import lax
from jax.experimental import pallas as pl
from jax.experimental.pallas import tpu as pltpu
from jax.sharding import PartitionSpec as P


def presum_kernel(index_ref, basis_ref, weighted_ref, out_ref, acc_ref):
    acc_ref[...] = jnp.zeros_like(acc_ref)

    def body(s, carry):
        target = index_ref[4 * s]
        left = index_ref[4 * s + 2]
        right = index_ref[4 * s + 3]
        tile = lax.dot_general(
            basis_ref[left],
            weighted_ref[right],
            (((0,), (0,)), ((), ())),
            preferred_element_type=jnp.float32,
        )
        acc_ref[target] += tile.astype(jnp.bfloat16).astype(jnp.float32)
        return carry

    lax.fori_loop(0, index_ref.shape[0] // 4, body, 0)
    out_ref[...] = acc_ref[...].astype(out_ref.dtype)


def presum_tiles(index_flat, basis, weighted, n_rows):
    blocks, points, block_size = basis.shape
    contribs = index_flat.shape[0] // 4
    return pl.pallas_call(
        presum_kernel,
        out_shape=jax.ShapeDtypeStruct((n_rows, block_size, block_size), jnp.bfloat16),
        in_specs=[
            pl.BlockSpec(memory_space=pltpu.SMEM),
            pl.BlockSpec(memory_space=pltpu.VMEM),
            pl.BlockSpec(memory_space=pltpu.VMEM),
        ],
        out_specs=pl.BlockSpec(memory_space=pltpu.VMEM),
        scratch_shapes=[pltpu.VMEM((n_rows, block_size, block_size), jnp.float32)],
        cost_estimate=pl.CostEstimate(
            flops=2 * contribs * points * block_size * block_size,
            transcendentals=0,
            bytes_accessed=2 * basis.size * 2 + n_rows * block_size * block_size * 2,
        ),
    )(index_flat, basis, weighted)


def on_device(
    basis_values, potential, contrib_index, pattern, ghost_list, state, damp_lower, damp_upper
):
    n_rows = lax.axis_size("rows")
    n_cols = lax.axis_size("cols")
    basis_blocks, points, block_size = basis_values.shape
    vec_count = state.shape[0]
    row_blocks = state.shape[1] // block_size
    group_slots = pattern.shape[1]
    slot_count = group_slots // n_cols
    ghost_width = ghost_list.shape[2]

    ghost_ids = ghost_list[0]
    owners = jnp.arange(n_rows, dtype=jnp.int32)[:, None] * row_blocks
    requested = jnp.where(ghost_ids >= 0, ghost_ids - owners, -1)
    target_row = contrib_index[:, 0]
    to_target = target_row[:, None] == jnp.arange(n_rows, dtype=jnp.int32)[None, :]
    slot_for_target = jnp.max(jnp.where(to_target, contrib_index[:, 1:2], -1), axis=0)
    index_send = jnp.concatenate([requested, slot_for_target[:, None]], axis=1)
    index_recv = lax.all_to_all(index_send, "rows", split_axis=0, concat_axis=0, tiled=True)
    wanted_by = index_recv[:, :ghost_width]
    arrived_slots = index_recv[:, ghost_width]

    center = (damp_upper[0] + damp_lower[0]) / 2.0
    half_width = (damp_upper[0] - damp_lower[0]) / 2.0

    def own_blocks(vectors):
        return (
            vectors.astype(jnp.bfloat16)
            .reshape(vec_count, row_blocks, block_size)
            .transpose(1, 0, 2)
        )

    def with_ghosts(blocks):
        outgoing = jnp.where(
            (wanted_by >= 0)[:, :, None, None],
            blocks[jnp.clip(wanted_by, 0, row_blocks - 1)],
            jnp.zeros((), jnp.bfloat16),
        )
        arrived = lax.all_to_all(outgoing, "rows", split_axis=0, concat_axis=0, tiled=True)
        return jnp.concatenate(
            [blocks, arrived.reshape(n_rows * ghost_width, vec_count, block_size)], axis=0
        )

    weighted = (basis_values.astype(jnp.float32) * potential[None, :, None]).astype(jnp.bfloat16)
    send_tiles = presum_tiles(contrib_index.reshape(-1), basis_values, weighted, n_rows)
    arrived_tiles = lax.all_to_all(send_tiles, "rows", split_axis=0, concat_axis=0, tiled=True)
    arrived_tiles, state_in = lax.optimization_barrier((arrived_tiles, state))
    state_pool = with_ghosts(own_blocks(state_in))
    slot_wanted = jnp.arange(slot_count, dtype=jnp.int32)
    selector = (arrived_slots[None, :] == slot_wanted[:, None]).astype(jnp.bfloat16)
    assembled = jnp.dot(
        selector,
        arrived_tiles.reshape(n_rows, block_size * block_size),
        preferred_element_type=jnp.float32,
    )
    assembled = assembled.astype(jnp.bfloat16).reshape(slot_count, block_size, block_size)
    group_tiles = lax.all_gather(assembled, "cols", axis=0, tiled=True)

    rows_local = pattern[0, :, 0]
    sources = pattern[0, :, 1]

    def accumulate(tile_part, source_part, row_part, operand_pool):
        operands = operand_pool[source_part]
        products = jnp.einsum(
            "kvb,kab->kva", operands, tile_part, preferred_element_type=jnp.float32
        )
        row_select = (row_part[:, None] == jnp.arange(row_blocks, dtype=jnp.int32)[None, :]).astype(
            jnp.float32
        )
        return jnp.einsum("ki,kva->iva", row_select, products, precision=lax.Precision.HIGHEST)

    def as_field(running):
        return running.transpose(1, 0, 2).reshape(vec_count, row_blocks * block_size)

    first_image = as_field(accumulate(group_tiles, sources, rows_local, state_pool))
    first_term = (first_image - center * state) / half_width
    first_pool = with_ghosts(own_blocks(first_term))
    second_image = as_field(accumulate(group_tiles, sources, rows_local, first_pool))
    second_term = 2.0 * (second_image - center * first_term) / half_width - state
    return (first_term, second_term)


def solution(mesh):
    in_specs = (
        P(("rows", "cols"), None, None),
        P(("rows", "cols")),
        P(("rows", "cols"), None),
        P("rows", None, None),
        P("rows", None, None),
        P("cols", "rows"),
        P(),
        P(),
    )
    out_specs = (P("cols", "rows"), P("cols", "rows"))
    return jax.shard_map(
        on_device, mesh=mesh, in_specs=in_specs, out_specs=out_specs, check_vma=False
    )
```

```python
import jax
import jax.numpy as jnp
from jax import lax
from jax.experimental import pallas as pl
from jax.experimental.pallas import tpu as pltpu
from jax.sharding import PartitionSpec as P


def presum_kernel(index_ref, stacked_ref, basis_ref, out_ref, tiles_ref, acc_ref):
    blocks, block_size = basis_ref.shape[0], basis_ref.shape[2]
    for left in range(blocks):
        product = jnp.dot(stacked_ref[...], basis_ref[left], preferred_element_type=jnp.float32)
        for right in range(blocks):
            tiles_ref[left, right] = product[right * block_size : (right + 1) * block_size].astype(
                jnp.bfloat16
            )
    acc_ref[...] = jnp.zeros_like(acc_ref)

    def body(s, carry):
        target = index_ref[4 * s]
        acc_ref[target] += tiles_ref[index_ref[4 * s + 2], index_ref[4 * s + 3]].astype(jnp.float32)
        return carry

    lax.fori_loop(0, index_ref.shape[0] // 4, body, 0)
    out_ref[...] = acc_ref[...].astype(out_ref.dtype)


def presum_tiles(index_flat, basis, weighted, n_rows):
    blocks, points, block_size = basis.shape
    stacked = weighted.transpose(0, 2, 1).reshape(blocks * block_size, points)
    return pl.pallas_call(
        presum_kernel,
        out_shape=jax.ShapeDtypeStruct((n_rows, block_size, block_size), jnp.bfloat16),
        in_specs=[
            pl.BlockSpec(memory_space=pltpu.SMEM),
            pl.BlockSpec(memory_space=pltpu.VMEM),
            pl.BlockSpec(memory_space=pltpu.VMEM),
        ],
        out_specs=pl.BlockSpec(memory_space=pltpu.VMEM),
        scratch_shapes=[
            pltpu.VMEM((blocks, blocks, block_size, block_size), jnp.bfloat16),
            pltpu.VMEM((n_rows, block_size, block_size), jnp.float32),
        ],
        cost_estimate=pl.CostEstimate(
            flops=2 * blocks * blocks * points * block_size * block_size,
            transcendentals=0,
            bytes_accessed=2 * basis.size * 2 + n_rows * block_size * block_size * 2,
        ),
    )(index_flat, stacked, basis)


def on_device(
    basis_values, potential, contrib_index, pattern, ghost_list, state, damp_lower, damp_upper
):
    n_rows = lax.axis_size("rows")
    n_cols = lax.axis_size("cols")
    basis_blocks, points, block_size = basis_values.shape
    vec_count = state.shape[0]
    row_blocks = state.shape[1] // block_size
    group_slots = pattern.shape[1]
    slot_count = group_slots // n_cols
    ghost_width = ghost_list.shape[2]

    ghost_ids = ghost_list[0]
    owners = jnp.arange(n_rows, dtype=jnp.int32)[:, None] * row_blocks
    requested = jnp.where(ghost_ids >= 0, ghost_ids - owners, -1)
    target_row = contrib_index[:, 0]
    to_target = target_row[:, None] == jnp.arange(n_rows, dtype=jnp.int32)[None, :]
    slot_for_target = jnp.max(jnp.where(to_target, contrib_index[:, 1:2], -1), axis=0)
    index_send = jnp.concatenate([requested, slot_for_target[:, None]], axis=1)
    index_recv = lax.all_to_all(index_send, "rows", split_axis=0, concat_axis=0, tiled=True)
    wanted_by = index_recv[:, :ghost_width]
    arrived_slots = index_recv[:, ghost_width]

    center = (damp_upper[0] + damp_lower[0]) / 2.0
    half_width = (damp_upper[0] - damp_lower[0]) / 2.0

    def own_blocks(vectors):
        return (
            vectors.astype(jnp.bfloat16)
            .reshape(vec_count, row_blocks, block_size)
            .transpose(1, 0, 2)
        )

    def with_ghosts(blocks):
        outgoing = jnp.where(
            (wanted_by >= 0)[:, :, None, None],
            blocks[jnp.clip(wanted_by, 0, row_blocks - 1)],
            jnp.zeros((), jnp.bfloat16),
        )
        arrived = lax.all_to_all(outgoing, "rows", split_axis=0, concat_axis=0, tiled=True)
        return jnp.concatenate(
            [blocks, arrived.reshape(n_rows * ghost_width, vec_count, block_size)], axis=0
        )

    weighted = (basis_values.astype(jnp.float32) * potential[None, :, None]).astype(jnp.bfloat16)
    send_tiles = presum_tiles(contrib_index.reshape(-1), basis_values, weighted, n_rows)
    arrived_tiles = lax.all_to_all(send_tiles, "rows", split_axis=0, concat_axis=0, tiled=True)
    arrived_tiles, state_in = lax.optimization_barrier((arrived_tiles, state))
    state_pool = with_ghosts(own_blocks(state_in))
    slot_wanted = jnp.arange(slot_count, dtype=jnp.int32)
    selector = (arrived_slots[None, :] == slot_wanted[:, None]).astype(jnp.bfloat16)
    assembled = jnp.dot(
        selector,
        arrived_tiles.reshape(n_rows, block_size * block_size),
        preferred_element_type=jnp.float32,
    )
    assembled = assembled.astype(jnp.bfloat16).reshape(slot_count, block_size, block_size)
    group_tiles = lax.all_gather(assembled, "cols", axis=0, tiled=True)

    rows_local = pattern[0, :, 0]
    sources = pattern[0, :, 1]

    def accumulate(tile_part, source_part, row_part, operand_pool):
        operands = operand_pool[source_part]
        products = jnp.einsum(
            "kvb,kba->kva", operands, tile_part, preferred_element_type=jnp.float32
        )
        row_select = (row_part[:, None] == jnp.arange(row_blocks, dtype=jnp.int32)[None, :]).astype(
            jnp.float32
        )
        return jnp.einsum("ki,kva->iva", row_select, products, precision=lax.Precision.HIGHEST)

    def as_field(running):
        return running.transpose(1, 0, 2).reshape(vec_count, row_blocks * block_size)

    first_image = as_field(accumulate(group_tiles, sources, rows_local, state_pool))
    first_term = (first_image - center * state) / half_width
    first_pool = with_ghosts(own_blocks(first_term))
    second_image = as_field(accumulate(group_tiles, sources, rows_local, first_pool))
    second_term = 2.0 * (second_image - center * first_term) / half_width - state
    return (first_term, second_term)


def solution(mesh):
    in_specs = (
        P(("rows", "cols"), None, None),
        P(("rows", "cols")),
        P(("rows", "cols"), None),
        P("rows", None, None),
        P("rows", None, None),
        P("cols", "rows"),
        P(),
        P(),
    )
    out_specs = (P("cols", "rows"), P("cols", "rows"))
    return jax.shard_map(
        on_device, mesh=mesh, in_specs=in_specs, out_specs=out_specs, check_vma=False
    )
```

```python
import jax
import jax.numpy as jnp
from jax import lax
from jax.experimental import pallas as pl
from jax.experimental.pallas import tpu as pltpu
from jax.sharding import PartitionSpec as P


def presum_kernel(index_ref, stacked_ref, basis_ref, out_ref, tiles_ref, acc_ref):
    blocks, block_size = basis_ref.shape[0], basis_ref.shape[2]
    for left in range(blocks):
        product = jnp.dot(stacked_ref[...], basis_ref[left], preferred_element_type=jnp.float32)
        for right in range(blocks):
            tiles_ref[left, right] = product[right * block_size : (right + 1) * block_size].astype(
                jnp.bfloat16
            )
    acc_ref[...] = jnp.zeros_like(acc_ref)

    def body(s, carry):
        target = index_ref[4 * s]
        acc_ref[target] += tiles_ref[index_ref[4 * s + 2], index_ref[4 * s + 3]].astype(jnp.float32)
        return carry

    lax.fori_loop(0, index_ref.shape[0] // 4, body, 0)
    out_ref[...] = acc_ref[...].astype(out_ref.dtype)


def presum_tiles(index_flat, basis, weighted, n_rows):
    blocks, points, block_size = basis.shape
    stacked = weighted.transpose(0, 2, 1).reshape(blocks * block_size, points)
    return pl.pallas_call(
        presum_kernel,
        out_shape=jax.ShapeDtypeStruct((n_rows, block_size, block_size), jnp.bfloat16),
        in_specs=[
            pl.BlockSpec(memory_space=pltpu.SMEM),
            pl.BlockSpec(memory_space=pltpu.VMEM),
            pl.BlockSpec(memory_space=pltpu.VMEM),
        ],
        out_specs=pl.BlockSpec(memory_space=pltpu.VMEM),
        scratch_shapes=[
            pltpu.VMEM((blocks, blocks, block_size, block_size), jnp.bfloat16),
            pltpu.VMEM((n_rows, block_size, block_size), jnp.float32),
        ],
        cost_estimate=pl.CostEstimate(
            flops=2 * blocks * blocks * points * block_size * block_size,
            transcendentals=0,
            bytes_accessed=2 * basis.size * 2 + n_rows * block_size * block_size * 2,
        ),
    )(index_flat, stacked, basis)


def product_kernel(pattern_ref, tiles_ref, local_ref, ghost_ref, out_ref, acc_ref):
    row_blocks, vec_count, block_size = local_ref.shape
    acc_ref[...] = jnp.zeros_like(acc_ref)

    def body(g, carry):
        row = pattern_ref[2 * g]
        source = pattern_ref[2 * g + 1]
        local = local_ref[jnp.minimum(source, row_blocks - 1)]
        ghost = ghost_ref[jnp.maximum(source - row_blocks, 0)]
        operand = jnp.where(source < row_blocks, local, ghost)
        acc_ref[row] += jnp.dot(operand, tiles_ref[g], preferred_element_type=jnp.float32)
        return carry

    lax.fori_loop(0, tiles_ref.shape[0], body, 0, unroll=8)
    for row in range(row_blocks):
        out_ref[:, row * block_size : (row + 1) * block_size] = acc_ref[row]


def apply_tiles(pattern_flat, tiles, local_blocks, ghost_blocks):
    row_blocks, vec_count, block_size = local_blocks.shape
    slots = tiles.shape[0]
    return pl.pallas_call(
        product_kernel,
        out_shape=jax.ShapeDtypeStruct((vec_count, row_blocks * block_size), jnp.float32),
        in_specs=[
            pl.BlockSpec(memory_space=pltpu.SMEM),
            pl.BlockSpec(memory_space=pltpu.VMEM),
            pl.BlockSpec(memory_space=pltpu.VMEM),
            pl.BlockSpec(memory_space=pltpu.VMEM),
        ],
        out_specs=pl.BlockSpec(memory_space=pltpu.VMEM),
        scratch_shapes=[pltpu.VMEM((row_blocks, vec_count, block_size), jnp.float32)],
        cost_estimate=pl.CostEstimate(
            flops=2 * slots * vec_count * block_size * block_size,
            transcendentals=0,
            bytes_accessed=tiles.size * 2 + ghost_blocks.size * 2 + vec_count * row_blocks * block_size * 4,
        ),
    )(pattern_flat, tiles, local_blocks, ghost_blocks)


def on_device(
    basis_values, potential, contrib_index, pattern, ghost_list, state, damp_lower, damp_upper
):
    n_rows = lax.axis_size("rows")
    n_cols = lax.axis_size("cols")
    basis_blocks, points, block_size = basis_values.shape
    vec_count = state.shape[0]
    row_blocks = state.shape[1] // block_size
    group_slots = pattern.shape[1]
    slot_count = group_slots // n_cols
    ghost_width = ghost_list.shape[2]

    ghost_ids = ghost_list[0]
    owners = jnp.arange(n_rows, dtype=jnp.int32)[:, None] * row_blocks
    requested = jnp.where(ghost_ids >= 0, ghost_ids - owners, -1)
    target_row = contrib_index[:, 0]
    to_target = target_row[:, None] == jnp.arange(n_rows, dtype=jnp.int32)[None, :]
    slot_for_target = jnp.max(jnp.where(to_target, contrib_index[:, 1:2], -1), axis=0)
    index_send = jnp.concatenate([requested, slot_for_target[:, None]], axis=1)
    index_recv = lax.all_to_all(index_send, "rows", split_axis=0, concat_axis=0, tiled=True)
    wanted_by = index_recv[:, :ghost_width]
    arrived_slots = index_recv[:, ghost_width]

    center = (damp_upper[0] + damp_lower[0]) / 2.0
    half_width = (damp_upper[0] - damp_lower[0]) / 2.0

    def own_blocks(vectors):
        return (
            vectors.astype(jnp.bfloat16)
            .reshape(vec_count, row_blocks, block_size)
            .transpose(1, 0, 2)
        )

    def ghosts_of(blocks):
        outgoing = jnp.where(
            (wanted_by >= 0)[:, :, None, None],
            blocks[jnp.clip(wanted_by, 0, row_blocks - 1)],
            jnp.zeros((), jnp.bfloat16),
        )
        arrived = lax.all_to_all(outgoing, "rows", split_axis=0, concat_axis=0, tiled=True)
        return arrived.reshape(n_rows * ghost_width, vec_count, block_size)

    weighted = (basis_values.astype(jnp.float32) * potential[None, :, None]).astype(jnp.bfloat16)
    send_tiles = presum_tiles(contrib_index.reshape(-1), basis_values, weighted, n_rows)
    arrived_tiles = lax.all_to_all(send_tiles, "rows", split_axis=0, concat_axis=0, tiled=True)
    arrived_tiles, state_in = lax.optimization_barrier((arrived_tiles, state))
    state_blocks = own_blocks(state_in)
    state_ghosts = ghosts_of(state_blocks)
    slot_wanted = jnp.arange(slot_count, dtype=jnp.int32)
    selector = (arrived_slots[None, :] == slot_wanted[:, None]).astype(jnp.bfloat16)
    assembled = jnp.dot(
        selector,
        arrived_tiles.reshape(n_rows, block_size * block_size),
        preferred_element_type=jnp.float32,
    )
    assembled = assembled.astype(jnp.bfloat16).reshape(slot_count, block_size, block_size)
    group_tiles = lax.all_gather(assembled, "cols", axis=0, tiled=True)

    pattern_flat = pattern.reshape(-1)
    first_image = apply_tiles(pattern_flat, group_tiles, state_blocks, state_ghosts)
    first_term = (first_image - center * state) / half_width
    first_blocks = own_blocks(first_term)
    second_image = apply_tiles(pattern_flat, group_tiles, first_blocks, ghosts_of(first_blocks))
    second_term = 2.0 * (second_image - center * first_term) / half_width - state
    return (first_term, second_term)


def solution(mesh):
    in_specs = (
        P(("rows", "cols"), None, None),
        P(("rows", "cols")),
        P(("rows", "cols"), None),
        P("rows", None, None),
        P("rows", None, None),
        P("cols", "rows"),
        P(),
        P(),
    )
    out_specs = (P("cols", "rows"), P("cols", "rows"))
    return jax.shard_map(
        on_device, mesh=mesh, in_specs=in_specs, out_specs=out_specs, check_vma=False
    )
```

```python
import jax
import jax.numpy as jnp
from jax import lax
from jax.experimental import pallas as pl
from jax.experimental.pallas import tpu as pltpu
from jax.sharding import PartitionSpec as P


def presum_kernel(index_ref, stacked_ref, basis_ref, out_ref, tiles_ref, acc_ref):
    blocks, block_size = basis_ref.shape[0], basis_ref.shape[2]
    for left in range(blocks):
        product = jnp.dot(stacked_ref[...], basis_ref[left], preferred_element_type=jnp.float32)
        for right in range(blocks):
            tiles_ref[left, right] = product[right * block_size : (right + 1) * block_size].astype(
                jnp.bfloat16
            )
    acc_ref[...] = jnp.zeros_like(acc_ref)

    def body(s, carry):
        target = index_ref[4 * s]
        acc_ref[target] += tiles_ref[index_ref[4 * s + 2], index_ref[4 * s + 3]].astype(jnp.float32)
        return carry

    lax.fori_loop(0, index_ref.shape[0] // 4, body, 0)
    out_ref[...] = acc_ref[...].astype(out_ref.dtype)


def presum_tiles(index_flat, basis, weighted, n_rows):
    blocks, points, block_size = basis.shape
    stacked = weighted.transpose(0, 2, 1).reshape(blocks * block_size, points)
    return pl.pallas_call(
        presum_kernel,
        out_shape=jax.ShapeDtypeStruct((n_rows, block_size, block_size), jnp.bfloat16),
        in_specs=[
            pl.BlockSpec(memory_space=pltpu.SMEM),
            pl.BlockSpec(memory_space=pltpu.VMEM),
            pl.BlockSpec(memory_space=pltpu.VMEM),
        ],
        out_specs=pl.BlockSpec(memory_space=pltpu.VMEM),
        scratch_shapes=[
            pltpu.VMEM((blocks, blocks, block_size, block_size), jnp.bfloat16),
            pltpu.VMEM((n_rows, block_size, block_size), jnp.float32),
        ],
        cost_estimate=pl.CostEstimate(
            flops=2 * blocks * blocks * points * block_size * block_size,
            transcendentals=0,
            bytes_accessed=2 * basis.size * 2 + n_rows * block_size * block_size * 2,
        ),
    )(index_flat, stacked, basis)


def product_kernel(pattern_ref, tiles_ref, local_ref, ghost_ref, out_ref, acc_ref):
    row_blocks, vec_count, block_size = local_ref.shape
    acc_ref[...] = jnp.zeros_like(acc_ref)

    def body(g, carry):
        row = pattern_ref[2 * g]
        source = pattern_ref[2 * g + 1]
        local = local_ref[jnp.minimum(source, row_blocks - 1)]
        ghost = ghost_ref[jnp.maximum(source - row_blocks, 0)]
        operand = jnp.where(source < row_blocks, local, ghost)
        acc_ref[row] += jnp.dot(operand, tiles_ref[g], preferred_element_type=jnp.float32)
        return carry

    lax.fori_loop(0, tiles_ref.shape[0], body, 0, unroll=8)
    for row in range(row_blocks):
        out_ref[:, row * block_size : (row + 1) * block_size] = acc_ref[row]


def apply_tiles(pattern_flat, tiles, local_blocks, ghost_blocks):
    row_blocks, vec_count, block_size = local_blocks.shape
    slots = tiles.shape[0]
    return pl.pallas_call(
        product_kernel,
        out_shape=jax.ShapeDtypeStruct((vec_count, row_blocks * block_size), jnp.float32),
        in_specs=[
            pl.BlockSpec(memory_space=pltpu.SMEM),
            pl.BlockSpec(memory_space=pltpu.VMEM),
            pl.BlockSpec(memory_space=pltpu.VMEM),
            pl.BlockSpec(memory_space=pltpu.VMEM),
        ],
        out_specs=pl.BlockSpec(memory_space=pltpu.VMEM),
        scratch_shapes=[pltpu.VMEM((row_blocks, vec_count, block_size), jnp.float32)],
        cost_estimate=pl.CostEstimate(
            flops=2 * slots * vec_count * block_size * block_size,
            transcendentals=0,
            bytes_accessed=tiles.size * 2 + ghost_blocks.size * 2 + vec_count * row_blocks * block_size * 4,
        ),
    )(pattern_flat, tiles, local_blocks, ghost_blocks)


def on_device(
    basis_values, potential, contrib_index, pattern, ghost_list, state, damp_lower, damp_upper
):
    n_rows = lax.axis_size("rows")
    n_cols = lax.axis_size("cols")
    basis_blocks, points, block_size = basis_values.shape
    vec_count = state.shape[0]
    row_blocks = state.shape[1] // block_size
    group_slots = pattern.shape[1]
    slot_count = group_slots // n_cols
    ghost_width = ghost_list.shape[2]

    ghost_ids = ghost_list[0]
    owners = jnp.arange(n_rows, dtype=jnp.int32)[:, None] * row_blocks
    requested = jnp.where(ghost_ids >= 0, ghost_ids - owners, -1)
    target_row = contrib_index[:, 0]
    to_target = target_row[:, None] == jnp.arange(n_rows, dtype=jnp.int32)[None, :]
    slot_for_target = jnp.max(jnp.where(to_target, contrib_index[:, 1:2], -1), axis=0)
    index_send = jnp.concatenate([requested, slot_for_target[:, None]], axis=1)
    index_all = lax.all_gather(index_send, "rows", axis=0)
    index_recv = lax.dynamic_index_in_dim(index_all, lax.axis_index("rows"), axis=1, keepdims=False)
    wanted_by = index_recv[:, :ghost_width]
    arrived_slots = index_recv[:, ghost_width]

    center = (damp_upper[0] + damp_lower[0]) / 2.0
    half_width = (damp_upper[0] - damp_lower[0]) / 2.0

    def own_blocks(vectors):
        return (
            vectors.astype(jnp.bfloat16)
            .reshape(vec_count, row_blocks, block_size)
            .transpose(1, 0, 2)
        )

    def ghosts_of(blocks):
        outgoing = jnp.where(
            (wanted_by >= 0)[:, :, None, None],
            blocks[jnp.clip(wanted_by, 0, row_blocks - 1)],
            jnp.zeros((), jnp.bfloat16),
        )
        arrived = lax.all_to_all(outgoing, "rows", split_axis=0, concat_axis=0, tiled=True)
        return arrived.reshape(n_rows * ghost_width, vec_count, block_size)

    weighted = (basis_values.astype(jnp.float32) * potential[None, :, None]).astype(jnp.bfloat16)
    send_tiles = presum_tiles(contrib_index.reshape(-1), basis_values, weighted, n_rows)
    arrived_tiles = lax.all_to_all(send_tiles, "rows", split_axis=0, concat_axis=0, tiled=True)
    arrived_tiles, state_in = lax.optimization_barrier((arrived_tiles, state))
    state_blocks = own_blocks(state_in)
    state_ghosts = ghosts_of(state_blocks)
    slot_wanted = jnp.arange(slot_count, dtype=jnp.int32)
    selector = (arrived_slots[None, :] == slot_wanted[:, None]).astype(jnp.bfloat16)
    assembled = jnp.dot(
        selector,
        arrived_tiles.reshape(n_rows, block_size * block_size),
        preferred_element_type=jnp.float32,
    )
    assembled = assembled.astype(jnp.bfloat16).reshape(slot_count, block_size, block_size)
    group_tiles = lax.all_gather(assembled, "cols", axis=0, tiled=True)

    pattern_flat = pattern.reshape(-1)
    first_image = apply_tiles(pattern_flat, group_tiles, state_blocks, state_ghosts)
    first_term = (first_image - center * state) / half_width
    first_blocks = own_blocks(first_term)
    second_image = apply_tiles(pattern_flat, group_tiles, first_blocks, ghosts_of(first_blocks))
    second_term = 2.0 * (second_image - center * first_term) / half_width - state
    return (first_term, second_term)


def solution(mesh):
    in_specs = (
        P(("rows", "cols"), None, None),
        P(("rows", "cols")),
        P(("rows", "cols"), None),
        P("rows", None, None),
        P("rows", None, None),
        P("cols", "rows"),
        P(),
        P(),
    )
    out_specs = (P("cols", "rows"), P("cols", "rows"))
    return jax.shard_map(
        on_device, mesh=mesh, in_specs=in_specs, out_specs=out_specs, check_vma=False
    )
```

```python
import functools

import jax
import jax.numpy as jnp
from jax import lax
from jax.experimental import pallas as pl
from jax.experimental.pallas import tpu as pltpu
from jax.sharding import PartitionSpec as P


def presum_kernel(index_ref, stacked_ref, basis_ref, out_ref, tiles_ref, acc_ref):
    blocks, block_size = basis_ref.shape[0], basis_ref.shape[2]
    for left in range(blocks):
        product = jnp.dot(stacked_ref[...], basis_ref[left], preferred_element_type=jnp.float32)
        for right in range(blocks):
            tiles_ref[left, right] = product[right * block_size : (right + 1) * block_size].astype(
                jnp.bfloat16
            )
    acc_ref[...] = jnp.zeros_like(acc_ref)

    def body(s, carry):
        target = index_ref[4 * s]
        acc_ref[target] += tiles_ref[index_ref[4 * s + 2], index_ref[4 * s + 3]].astype(jnp.float32)
        return carry

    lax.fori_loop(0, index_ref.shape[0] // 4, body, 0, unroll=8)
    out_ref[...] = acc_ref[...].astype(out_ref.dtype)


def presum_tiles(index_flat, basis, weighted, n_rows):
    blocks, points, block_size = basis.shape
    stacked = weighted.transpose(0, 2, 1).reshape(blocks * block_size, points)
    return pl.pallas_call(
        presum_kernel,
        out_shape=jax.ShapeDtypeStruct((n_rows, block_size, block_size), jnp.bfloat16),
        in_specs=[
            pl.BlockSpec(memory_space=pltpu.SMEM),
            pl.BlockSpec(memory_space=pltpu.VMEM),
            pl.BlockSpec(memory_space=pltpu.VMEM),
        ],
        out_specs=pl.BlockSpec(memory_space=pltpu.VMEM),
        scratch_shapes=[
            pltpu.VMEM((blocks, blocks, block_size, block_size), jnp.bfloat16),
            pltpu.VMEM((n_rows, block_size, block_size), jnp.float32),
        ],
        cost_estimate=pl.CostEstimate(
            flops=2 * blocks * blocks * points * block_size * block_size,
            transcendentals=0,
            bytes_accessed=2 * basis.size * 2 + n_rows * block_size * block_size * 2,
        ),
    )(index_flat, stacked, basis)


def product_kernel(first, pattern_ref, scalar_ref, tiles_ref, local_ref, ghost_ref, *refs):
    row_blocks, vec_count, block_size = local_ref.shape
    acc_ref = refs[-1]
    acc_ref[...] = jnp.zeros_like(acc_ref)

    def body(g, carry):
        row = pattern_ref[2 * g]
        source = pattern_ref[2 * g + 1]
        local = local_ref[jnp.minimum(source, row_blocks - 1)]
        ghost = ghost_ref[jnp.maximum(source - row_blocks, 0)]
        operand = jnp.where(source < row_blocks, local, ghost)
        acc_ref[row] += jnp.dot(operand, tiles_ref[g], preferred_element_type=jnp.float32)
        return carry

    lax.fori_loop(0, tiles_ref.shape[0], body, 0, unroll=8)
    center = scalar_ref[0]
    half_width = scalar_ref[1]
    if first:
        state_ref, out_ref, blocks_ref = refs[0], refs[1], refs[2]
        for row in range(row_blocks):
            lanes = slice(row * block_size, (row + 1) * block_size)
            term = (acc_ref[row] - center * state_ref[:, lanes]) / half_width
            out_ref[:, lanes] = term
            blocks_ref[row] = term.astype(blocks_ref.dtype)
    else:
        first_ref, state_ref, out_ref = refs[0], refs[1], refs[2]
        for row in range(row_blocks):
            lanes = slice(row * block_size, (row + 1) * block_size)
            out_ref[:, lanes] = (
                2.0 * (acc_ref[row] - center * first_ref[:, lanes]) / half_width
                - state_ref[:, lanes]
            )


def apply_tiles(pattern_flat, scalars, tiles, local_blocks, ghost_blocks, fields):
    row_blocks, vec_count, block_size = local_blocks.shape
    slots = tiles.shape[0]
    field = jax.ShapeDtypeStruct((vec_count, row_blocks * block_size), jnp.float32)
    if len(fields) == 1:
        out_shape = (field, jax.ShapeDtypeStruct(local_blocks.shape, jnp.bfloat16))
    else:
        out_shape = field
    vmem = pl.BlockSpec(memory_space=pltpu.VMEM)
    smem = pl.BlockSpec(memory_space=pltpu.SMEM)
    return pl.pallas_call(
        functools.partial(product_kernel, len(fields) == 1),
        out_shape=out_shape,
        in_specs=[smem, smem] + [vmem] * (3 + len(fields)),
        out_specs=(vmem, vmem) if len(fields) == 1 else vmem,
        scratch_shapes=[pltpu.VMEM((row_blocks, vec_count, block_size), jnp.float32)],
        cost_estimate=pl.CostEstimate(
            flops=2 * slots * vec_count * block_size * block_size,
            transcendentals=0,
            bytes_accessed=tiles.size * 2 + ghost_blocks.size * 2 + 3 * field.size * 4,
        ),
    )(pattern_flat, scalars, tiles, local_blocks, ghost_blocks, *fields)


def on_device(
    basis_values, potential, contrib_index, pattern, ghost_list, state, damp_lower, damp_upper
):
    n_rows = lax.axis_size("rows")
    n_cols = lax.axis_size("cols")
    basis_blocks, points, block_size = basis_values.shape
    vec_count = state.shape[0]
    row_blocks = state.shape[1] // block_size
    group_slots = pattern.shape[1]
    slot_count = group_slots // n_cols
    ghost_width = ghost_list.shape[2]

    ghost_ids = ghost_list[0]
    owners = jnp.arange(n_rows, dtype=jnp.int32)[:, None] * row_blocks
    requested = jnp.where(ghost_ids >= 0, ghost_ids - owners, -1)
    target_row = contrib_index[:, 0]
    to_target = target_row[:, None] == jnp.arange(n_rows, dtype=jnp.int32)[None, :]
    slot_for_target = jnp.max(jnp.where(to_target, contrib_index[:, 1:2], -1), axis=0)
    index_send = jnp.concatenate([requested, slot_for_target[:, None]], axis=1)
    index_recv = lax.all_to_all(index_send, "rows", split_axis=0, concat_axis=0, tiled=True)
    wanted_by = index_recv[:, :ghost_width]
    arrived_slots = index_recv[:, ghost_width]

    center = (damp_upper[0] + damp_lower[0]) / 2.0
    half_width = (damp_upper[0] - damp_lower[0]) / 2.0

    def own_blocks(vectors):
        return (
            vectors.astype(jnp.bfloat16)
            .reshape(vec_count, row_blocks, block_size)
            .transpose(1, 0, 2)
        )

    def ghosts_of(blocks):
        outgoing = jnp.where(
            (wanted_by >= 0)[:, :, None, None],
            blocks[jnp.clip(wanted_by, 0, row_blocks - 1)],
            jnp.zeros((), jnp.bfloat16),
        )
        arrived = lax.all_to_all(outgoing, "rows", split_axis=0, concat_axis=0, tiled=True)
        return arrived.reshape(n_rows * ghost_width, vec_count, block_size)

    weighted = (basis_values.astype(jnp.float32) * potential[None, :, None]).astype(jnp.bfloat16)
    send_tiles = presum_tiles(contrib_index.reshape(-1), basis_values, weighted, n_rows)
    arrived_tiles = lax.all_to_all(send_tiles, "rows", split_axis=0, concat_axis=0, tiled=True)
    arrived_tiles, state_in = lax.optimization_barrier((arrived_tiles, state))
    state_blocks = own_blocks(state_in)
    state_ghosts = ghosts_of(state_blocks)
    slot_wanted = jnp.arange(slot_count, dtype=jnp.int32)
    selector = (arrived_slots[None, :] == slot_wanted[:, None]).astype(jnp.bfloat16)
    assembled = jnp.dot(
        selector,
        arrived_tiles.reshape(n_rows, block_size * block_size),
        preferred_element_type=jnp.float32,
    )
    assembled = assembled.astype(jnp.bfloat16).reshape(slot_count, block_size, block_size)
    group_tiles = lax.all_gather(assembled, "cols", axis=0, tiled=True)

    pattern_flat = pattern.reshape(-1)
    scalars = jnp.stack([center, half_width])
    first_term, first_blocks = apply_tiles(
        pattern_flat, scalars, group_tiles, state_blocks, state_ghosts, (state,)
    )
    second_term = apply_tiles(
        pattern_flat, scalars, group_tiles, first_blocks, ghosts_of(first_blocks), (first_term, state)
    )
    return (first_term, second_term)


def solution(mesh):
    in_specs = (
        P(("rows", "cols"), None, None),
        P(("rows", "cols")),
        P(("rows", "cols"), None),
        P("rows", None, None),
        P("rows", None, None),
        P("cols", "rows"),
        P(),
        P(),
    )
    out_specs = (P("cols", "rows"), P("cols", "rows"))
    return jax.shard_map(
        on_device, mesh=mesh, in_specs=in_specs, out_specs=out_specs, check_vma=False
    )
```

```python
import functools

import jax
import jax.numpy as jnp
from jax import lax
from jax.experimental import pallas as pl
from jax.experimental.pallas import tpu as pltpu
from jax.sharding import PartitionSpec as P


def presum_kernel(index_ref, stacked_ref, basis_ref, out_ref, tiles_ref, acc_ref):
    blocks, block_size = basis_ref.shape[0], basis_ref.shape[2]
    for left in range(blocks):
        product = jnp.dot(stacked_ref[...], basis_ref[left], preferred_element_type=jnp.float32)
        for right in range(blocks):
            tiles_ref[left, right] = product[right * block_size : (right + 1) * block_size].astype(
                jnp.bfloat16
            )
    acc_ref[...] = jnp.zeros_like(acc_ref)

    def body(s, carry):
        target = index_ref[4 * s]
        acc_ref[target] += tiles_ref[index_ref[4 * s + 2], index_ref[4 * s + 3]].astype(jnp.float32)
        return carry

    lax.fori_loop(0, index_ref.shape[0] // 4, body, 0, unroll=8)
    out_ref[...] = acc_ref[...].astype(out_ref.dtype)


def presum_tiles(index_flat, basis, weighted, n_rows):
    blocks, points, block_size = basis.shape
    stacked = weighted.transpose(0, 2, 1).reshape(blocks * block_size, points)
    return pl.pallas_call(
        presum_kernel,
        out_shape=jax.ShapeDtypeStruct((n_rows, block_size, block_size), jnp.bfloat16),
        in_specs=[
            pl.BlockSpec(memory_space=pltpu.SMEM),
            pl.BlockSpec(memory_space=pltpu.VMEM),
            pl.BlockSpec(memory_space=pltpu.VMEM),
        ],
        out_specs=pl.BlockSpec(memory_space=pltpu.VMEM),
        scratch_shapes=[
            pltpu.VMEM((blocks, blocks, block_size, block_size), jnp.bfloat16),
            pltpu.VMEM((n_rows, block_size, block_size), jnp.float32),
        ],
        cost_estimate=pl.CostEstimate(
            flops=2 * blocks * blocks * points * block_size * block_size,
            transcendentals=0,
            bytes_accessed=2 * basis.size * 2 + n_rows * block_size * block_size * 2,
        ),
    )(index_flat, stacked, basis)


def product_kernel(first, pattern_ref, scalar_ref, tiles_ref, local_ref, ghost_ref, *refs):
    row_blocks, vec_count, block_size = local_ref.shape
    acc_ref = refs[-1]
    acc_ref[...] = jnp.zeros_like(acc_ref)

    def body(g, carry):
        row = pattern_ref[3 * g]
        source = pattern_ref[3 * g + 1]
        local = local_ref[jnp.minimum(source, row_blocks - 1)]
        ghost = ghost_ref[jnp.maximum(source - row_blocks, 0)]
        operand = jnp.where(source < row_blocks, local, ghost)
        acc_ref[row] += jnp.dot(
            operand, tiles_ref[pattern_ref[3 * g + 2]], preferred_element_type=jnp.float32
        )
        return carry

    lax.fori_loop(0, tiles_ref.shape[0], body, 0, unroll=8)
    center = scalar_ref[0]
    half_width = scalar_ref[1]
    if first:
        state_ref, out_ref, blocks_ref = refs[0], refs[1], refs[2]
        for row in range(row_blocks):
            lanes = slice(row * block_size, (row + 1) * block_size)
            term = (acc_ref[row] - center * state_ref[:, lanes]) / half_width
            out_ref[:, lanes] = term
            blocks_ref[row] = term.astype(blocks_ref.dtype)
    else:
        first_ref, state_ref, out_ref = refs[0], refs[1], refs[2]
        for row in range(row_blocks):
            lanes = slice(row * block_size, (row + 1) * block_size)
            out_ref[:, lanes] = (
                2.0 * (acc_ref[row] - center * first_ref[:, lanes]) / half_width
                - state_ref[:, lanes]
            )


def apply_tiles(pattern_flat, scalars, tiles, local_blocks, ghost_blocks, fields):
    row_blocks, vec_count, block_size = local_blocks.shape
    slots = tiles.shape[0]
    field = jax.ShapeDtypeStruct((vec_count, row_blocks * block_size), jnp.float32)
    if len(fields) == 1:
        out_shape = (field, jax.ShapeDtypeStruct(local_blocks.shape, jnp.bfloat16))
    else:
        out_shape = field
    vmem = pl.BlockSpec(memory_space=pltpu.VMEM)
    smem = pl.BlockSpec(memory_space=pltpu.SMEM)
    return pl.pallas_call(
        functools.partial(product_kernel, len(fields) == 1),
        out_shape=out_shape,
        in_specs=[smem, smem] + [vmem] * (3 + len(fields)),
        out_specs=(vmem, vmem) if len(fields) == 1 else vmem,
        scratch_shapes=[pltpu.VMEM((row_blocks, vec_count, block_size), jnp.float32)],
        cost_estimate=pl.CostEstimate(
            flops=2 * slots * vec_count * block_size * block_size,
            transcendentals=0,
            bytes_accessed=tiles.size * 2 + ghost_blocks.size * 2 + 3 * field.size * 4,
        ),
    )(pattern_flat, scalars, tiles, local_blocks, ghost_blocks, *fields)


def on_device(
    basis_values, potential, contrib_index, pattern, ghost_list, state, damp_lower, damp_upper
):
    n_rows = lax.axis_size("rows")
    n_cols = lax.axis_size("cols")
    basis_blocks, points, block_size = basis_values.shape
    vec_count = state.shape[0]
    row_blocks = state.shape[1] // block_size
    group_slots = pattern.shape[1]
    slot_count = group_slots // n_cols
    ghost_width = ghost_list.shape[2]

    ghost_ids = ghost_list[0]
    owners = jnp.arange(n_rows, dtype=jnp.int32)[:, None] * row_blocks
    requested = jnp.where(ghost_ids >= 0, ghost_ids - owners, -1)
    target_row = contrib_index[:, 0]
    to_target = target_row[:, None] == jnp.arange(n_rows, dtype=jnp.int32)[None, :]
    slot_for_target = jnp.max(jnp.where(to_target, contrib_index[:, 1:2], -1), axis=0)
    index_send = jnp.concatenate([requested, slot_for_target[:, None]], axis=1)
    index_recv = lax.all_to_all(index_send, "rows", split_axis=0, concat_axis=0, tiled=True)
    wanted_by = index_recv[:, :ghost_width]
    arrived_slots = index_recv[:, ghost_width]

    center = (damp_upper[0] + damp_lower[0]) / 2.0
    half_width = (damp_upper[0] - damp_lower[0]) / 2.0

    def own_blocks(vectors):
        return (
            vectors.astype(jnp.bfloat16)
            .reshape(vec_count, row_blocks, block_size)
            .transpose(1, 0, 2)
        )

    def ghosts_of(blocks):
        outgoing = jnp.where(
            (wanted_by >= 0)[:, :, None, None],
            blocks[jnp.clip(wanted_by, 0, row_blocks - 1)],
            jnp.zeros((), jnp.bfloat16),
        )
        arrived = lax.all_to_all(outgoing, "rows", split_axis=0, concat_axis=0, tiled=True)
        return arrived.reshape(n_rows * ghost_width, vec_count, block_size)

    weighted = (basis_values.astype(jnp.float32) * potential[None, :, None]).astype(jnp.bfloat16)
    send_tiles = presum_tiles(contrib_index.reshape(-1), basis_values, weighted, n_rows)
    arrived_tiles = lax.all_to_all(send_tiles, "rows", split_axis=0, concat_axis=0, tiled=True)
    arrived_tiles, state_in = lax.optimization_barrier((arrived_tiles, state))
    state_blocks = own_blocks(state_in)
    state_ghosts = ghosts_of(state_blocks)
    slot_wanted = jnp.arange(slot_count, dtype=jnp.int32)
    selector = (arrived_slots[None, :] == slot_wanted[:, None]).astype(jnp.bfloat16)
    assembled = jnp.dot(
        selector,
        arrived_tiles.reshape(n_rows, block_size * block_size),
        preferred_element_type=jnp.float32,
    )
    assembled = assembled.astype(jnp.bfloat16).reshape(slot_count, block_size, block_size)
    shifted = [assembled] + [
        lax.ppermute(assembled, "cols", [(i, (i + k) % n_cols) for i in range(n_cols)])
        for k in range(1, n_cols)
    ]
    group_tiles = jnp.concatenate(shifted, axis=0)
    slot_ids = jnp.arange(group_slots, dtype=jnp.int32)
    shift_of = (lax.axis_index("cols") - slot_ids // slot_count) % n_cols
    tile_index = shift_of * slot_count + slot_ids % slot_count

    pattern_flat = jnp.concatenate([pattern[0], tile_index[:, None]], axis=1).reshape(-1)
    scalars = jnp.stack([center, half_width])
    first_term, first_blocks = apply_tiles(
        pattern_flat, scalars, group_tiles, state_blocks, state_ghosts, (state,)
    )
    second_term = apply_tiles(
        pattern_flat, scalars, group_tiles, first_blocks, ghosts_of(first_blocks), (first_term, state)
    )
    return (first_term, second_term)


def solution(mesh):
    in_specs = (
        P(("rows", "cols"), None, None),
        P(("rows", "cols")),
        P(("rows", "cols"), None),
        P("rows", None, None),
        P("rows", None, None),
        P("cols", "rows"),
        P(),
        P(),
    )
    out_specs = (P("cols", "rows"), P("cols", "rows"))
    return jax.shard_map(
        on_device, mesh=mesh, in_specs=in_specs, out_specs=out_specs, check_vma=False
    )
```

```python
import functools

import jax
import jax.numpy as jnp
from jax import lax
from jax.experimental import pallas as pl
from jax.experimental.pallas import tpu as pltpu
from jax.sharding import PartitionSpec as P


def presum_kernel(index_ref, stacked_ref, basis_ref, out_ref, tiles_ref, acc_ref):
    blocks, block_size = basis_ref.shape[0], basis_ref.shape[2]
    for left in range(blocks):
        product = jnp.dot(stacked_ref[...], basis_ref[left], preferred_element_type=jnp.float32)
        for right in range(blocks):
            tiles_ref[left, right] = product[right * block_size : (right + 1) * block_size].astype(
                jnp.bfloat16
            )
    acc_ref[...] = jnp.zeros_like(acc_ref)

    def body(s, carry):
        target = index_ref[4 * s]
        acc_ref[target] += tiles_ref[index_ref[4 * s + 2], index_ref[4 * s + 3]].astype(jnp.float32)
        return carry

    lax.fori_loop(0, index_ref.shape[0] // 4, body, 0, unroll=8)
    out_ref[...] = acc_ref[...].astype(out_ref.dtype)


def presum_tiles(index_flat, basis, weighted, n_rows):
    blocks, points, block_size = basis.shape
    stacked = weighted.transpose(0, 2, 1).reshape(blocks * block_size, points)
    return pl.pallas_call(
        presum_kernel,
        out_shape=jax.ShapeDtypeStruct((n_rows, block_size, block_size), jnp.bfloat16),
        in_specs=[
            pl.BlockSpec(memory_space=pltpu.SMEM),
            pl.BlockSpec(memory_space=pltpu.VMEM),
            pl.BlockSpec(memory_space=pltpu.VMEM),
        ],
        out_specs=pl.BlockSpec(memory_space=pltpu.VMEM),
        scratch_shapes=[
            pltpu.VMEM((blocks, blocks, block_size, block_size), jnp.bfloat16),
            pltpu.VMEM((n_rows, block_size, block_size), jnp.float32),
        ],
        cost_estimate=pl.CostEstimate(
            flops=2 * blocks * blocks * points * block_size * block_size,
            transcendentals=0,
            bytes_accessed=2 * basis.size * 2 + n_rows * block_size * block_size * 2,
        ),
    )(index_flat, stacked, basis)


def product_kernel(first, pattern_ref, scalar_ref, tiles_ref, local_ref, ghost_ref, *refs):
    row_blocks, vec_count, block_size = local_ref.shape
    acc_ref = refs[-1]
    acc_ref[...] = jnp.zeros_like(acc_ref)

    def body(g, carry):
        row = pattern_ref[3 * g]
        source = pattern_ref[3 * g + 1]
        local = local_ref[jnp.minimum(source, row_blocks - 1)]
        ghost = ghost_ref[jnp.maximum(source - row_blocks, 0)]
        operand = jnp.where(source < row_blocks, local, ghost)
        acc_ref[row] += jnp.dot(
            operand, tiles_ref[pattern_ref[3 * g + 2]], preferred_element_type=jnp.float32
        )
        return carry

    lax.fori_loop(0, tiles_ref.shape[0], body, 0, unroll=8)
    center = scalar_ref[0]
    half_width = scalar_ref[1]
    if first:
        state_ref, out_ref, blocks_ref = refs[0], refs[1], refs[2]
        for row in range(row_blocks):
            lanes = slice(row * block_size, (row + 1) * block_size)
            term = (acc_ref[row] - center * state_ref[:, lanes]) / half_width
            out_ref[:, lanes] = term
            blocks_ref[row] = term.astype(blocks_ref.dtype)
    else:
        first_ref, state_ref, out_ref = refs[0], refs[1], refs[2]
        for row in range(row_blocks):
            lanes = slice(row * block_size, (row + 1) * block_size)
            out_ref[:, lanes] = (
                2.0 * (acc_ref[row] - center * first_ref[:, lanes]) / half_width
                - state_ref[:, lanes]
            )


def apply_tiles(pattern_flat, scalars, tiles, local_blocks, ghost_blocks, fields):
    row_blocks, vec_count, block_size = local_blocks.shape
    slots = tiles.shape[0]
    field = jax.ShapeDtypeStruct((vec_count, row_blocks * block_size), jnp.float32)
    if len(fields) == 1:
        out_shape = (field, jax.ShapeDtypeStruct(local_blocks.shape, jnp.bfloat16))
    else:
        out_shape = field
    vmem = pl.BlockSpec(memory_space=pltpu.VMEM)
    smem = pl.BlockSpec(memory_space=pltpu.SMEM)
    return pl.pallas_call(
        functools.partial(product_kernel, len(fields) == 1),
        out_shape=out_shape,
        in_specs=[smem, smem] + [vmem] * (3 + len(fields)),
        out_specs=(vmem, vmem) if len(fields) == 1 else vmem,
        scratch_shapes=[pltpu.VMEM((row_blocks, vec_count, block_size), jnp.float32)],
        cost_estimate=pl.CostEstimate(
            flops=2 * slots * vec_count * block_size * block_size,
            transcendentals=0,
            bytes_accessed=tiles.size * 2 + ghost_blocks.size * 2 + 3 * field.size * 4,
        ),
    )(pattern_flat, scalars, tiles, local_blocks, ghost_blocks, *fields)


def on_device(
    basis_values, potential, contrib_index, pattern, ghost_list, state, damp_lower, damp_upper
):
    n_rows = lax.axis_size("rows")
    n_cols = lax.axis_size("cols")
    basis_blocks, points, block_size = basis_values.shape
    vec_count = state.shape[0]
    row_blocks = state.shape[1] // block_size
    group_slots = pattern.shape[1]
    slot_count = group_slots // n_cols
    ghost_width = ghost_list.shape[2]

    ghost_ids = ghost_list[0]
    owners = jnp.arange(n_rows, dtype=jnp.int32)[:, None] * row_blocks
    requested = jnp.where(ghost_ids >= 0, ghost_ids - owners, -1)
    target_row = contrib_index[:, 0]
    to_target = target_row[:, None] == jnp.arange(n_rows, dtype=jnp.int32)[None, :]
    slot_for_target = jnp.max(jnp.where(to_target, contrib_index[:, 1:2], -1), axis=0)
    index_send = jnp.concatenate([requested, slot_for_target[:, None]], axis=1)
    index_recv = lax.all_to_all(index_send, "rows", split_axis=0, concat_axis=0, tiled=True)
    wanted_by = index_recv[:, :ghost_width]
    arrived_slots = index_recv[:, ghost_width]

    center = (damp_upper[0] + damp_lower[0]) / 2.0
    half_width = (damp_upper[0] - damp_lower[0]) / 2.0

    def own_blocks(vectors):
        return (
            vectors.astype(jnp.bfloat16)
            .reshape(vec_count, row_blocks, block_size)
            .transpose(1, 0, 2)
        )

    def ghosts_of(blocks):
        outgoing = jnp.where(
            (wanted_by >= 0)[:, :, None, None],
            blocks[jnp.clip(wanted_by, 0, row_blocks - 1)],
            jnp.zeros((), jnp.bfloat16),
        )
        arrived = lax.all_to_all(outgoing, "rows", split_axis=0, concat_axis=0, tiled=True)
        return arrived.reshape(n_rows * ghost_width, vec_count, block_size)

    weighted = (basis_values.astype(jnp.float32) * potential[None, :, None]).astype(jnp.bfloat16)
    send_tiles = presum_tiles(contrib_index.reshape(-1), basis_values, weighted, n_rows)
    arrived_tiles = lax.all_to_all(send_tiles, "rows", split_axis=0, concat_axis=0, tiled=True)
    arrived_tiles, state_in = lax.optimization_barrier((arrived_tiles, state))
    state_blocks = own_blocks(state_in)
    state_ghosts = ghosts_of(state_blocks)
    slot_wanted = jnp.arange(slot_count, dtype=jnp.int32)
    selector = (arrived_slots[None, :] == slot_wanted[:, None]).astype(jnp.bfloat16)
    assembled = jnp.dot(
        selector,
        arrived_tiles.reshape(n_rows, block_size * block_size),
        preferred_element_type=jnp.float32,
    )
    assembled = assembled.astype(jnp.bfloat16).reshape(slot_count, block_size, block_size)
    group_tiles = assembled
    step = 1
    while step < n_cols:
        partner = [(i, i ^ step) for i in range(n_cols)]
        group_tiles = jnp.concatenate(
            [group_tiles, lax.ppermute(group_tiles, "cols", partner)], axis=0
        )
        step *= 2
    slot_ids = jnp.arange(group_slots, dtype=jnp.int32)
    shift_of = lax.bitwise_xor(lax.axis_index("cols"), slot_ids // slot_count)
    tile_index = shift_of * slot_count + slot_ids % slot_count

    pattern_flat = jnp.concatenate([pattern[0], tile_index[:, None]], axis=1).reshape(-1)
    scalars = jnp.stack([center, half_width])
    first_term, first_blocks = apply_tiles(
        pattern_flat, scalars, group_tiles, state_blocks, state_ghosts, (state,)
    )
    second_term = apply_tiles(
        pattern_flat, scalars, group_tiles, first_blocks, ghosts_of(first_blocks), (first_term, state)
    )
    return (first_term, second_term)


def solution(mesh):
    in_specs = (
        P(("rows", "cols"), None, None),
        P(("rows", "cols")),
        P(("rows", "cols"), None),
        P("rows", None, None),
        P("rows", None, None),
        P("cols", "rows"),
        P(),
        P(),
    )
    out_specs = (P("cols", "rows"), P("cols", "rows"))
    return jax.shard_map(
        on_device, mesh=mesh, in_specs=in_specs, out_specs=out_specs, check_vma=False
    )
```

```python
import functools

import jax
import jax.numpy as jnp
from jax import lax
from jax.experimental import pallas as pl
from jax.experimental.pallas import tpu as pltpu
from jax.sharding import PartitionSpec as P


def presum_kernel(index_ref, stacked_ref, basis_ref, out_ref, tiles_ref, acc_ref):
    blocks, block_size = basis_ref.shape[0], basis_ref.shape[2]
    for left in range(blocks):
        product = jnp.dot(stacked_ref[...], basis_ref[left], preferred_element_type=jnp.float32)
        for right in range(blocks):
            tiles_ref[left, right] = product[right * block_size : (right + 1) * block_size].astype(
                jnp.bfloat16
            )
    acc_ref[...] = jnp.zeros_like(acc_ref)

    def body(s, carry):
        target = index_ref[4 * s]
        acc_ref[target] += tiles_ref[index_ref[4 * s + 2], index_ref[4 * s + 3]].astype(jnp.float32)
        return carry

    lax.fori_loop(0, index_ref.shape[0] // 4, body, 0, unroll=8)
    out_ref[...] = acc_ref[...].astype(out_ref.dtype)


def presum_tiles(index_flat, basis, weighted, n_rows):
    blocks, points, block_size = basis.shape
    stacked = weighted.transpose(0, 2, 1).reshape(blocks * block_size, points)
    return pl.pallas_call(
        presum_kernel,
        out_shape=jax.ShapeDtypeStruct((n_rows, block_size, block_size), jnp.bfloat16),
        in_specs=[
            pl.BlockSpec(memory_space=pltpu.SMEM),
            pl.BlockSpec(memory_space=pltpu.VMEM),
            pl.BlockSpec(memory_space=pltpu.VMEM),
        ],
        out_specs=pl.BlockSpec(memory_space=pltpu.VMEM),
        scratch_shapes=[
            pltpu.VMEM((blocks, blocks, block_size, block_size), jnp.bfloat16),
            pltpu.VMEM((n_rows, block_size, block_size), jnp.float32),
        ],
        cost_estimate=pl.CostEstimate(
            flops=2 * blocks * blocks * points * block_size * block_size,
            transcendentals=0,
            bytes_accessed=2 * basis.size * 2 + n_rows * block_size * block_size * 2,
        ),
    )(index_flat, stacked, basis)


def product_kernel(first, pattern_ref, scalar_ref, tiles_ref, local_ref, ghost_ref, *refs):
    row_blocks, vec_count, block_size = local_ref.shape
    acc_ref = refs[-1]
    acc_ref[...] = jnp.zeros_like(acc_ref)

    def body(g, carry):
        row = pattern_ref[2 * g]
        source = pattern_ref[2 * g + 1]
        local = local_ref[jnp.minimum(source, row_blocks - 1)]
        ghost = ghost_ref[jnp.maximum(source - row_blocks, 0)]
        operand = jnp.where(source < row_blocks, local, ghost)
        acc_ref[row] += jnp.dot(operand, tiles_ref[g], preferred_element_type=jnp.float32)
        return carry

    lax.fori_loop(0, tiles_ref.shape[0], body, 0, unroll=8)
    center = scalar_ref[0]
    half_width = scalar_ref[1]
    if first:
        state_ref, wanted_ref, out_ref, blocks_ref, outgoing_ref = refs[:5]
        for row in range(row_blocks):
            lanes = slice(row * block_size, (row + 1) * block_size)
            term = (acc_ref[row] - center * state_ref[:, lanes]) / half_width
            out_ref[:, lanes] = term
            blocks_ref[row] = term.astype(blocks_ref.dtype)
        width = outgoing_ref.shape[1]

        def send(e, carry):
            wanted = wanted_ref[e]
            block = blocks_ref[jnp.clip(wanted, 0, row_blocks - 1)]
            outgoing_ref[e // width, e % width] = jnp.where(wanted >= 0, block, jnp.zeros_like(block))
            return carry

        lax.fori_loop(0, wanted_ref.shape[0], send, 0, unroll=8)
    else:
        first_ref, state_ref, out_ref = refs[0], refs[1], refs[2]
        for row in range(row_blocks):
            lanes = slice(row * block_size, (row + 1) * block_size)
            out_ref[:, lanes] = (
                2.0 * (acc_ref[row] - center * first_ref[:, lanes]) / half_width
                - state_ref[:, lanes]
            )


def apply_tiles(pattern_flat, scalars, tiles, local_blocks, ghost_blocks, fields, width, first=True):
    row_blocks, vec_count, block_size = local_blocks.shape
    slots = tiles.shape[0]
    field = jax.ShapeDtypeStruct((vec_count, row_blocks * block_size), jnp.float32)
    vmem = pl.BlockSpec(memory_space=pltpu.VMEM)
    smem = pl.BlockSpec(memory_space=pltpu.SMEM)
    if first:
        peers = fields[1].shape[0] // width
        out_shape = (
            field,
            jax.ShapeDtypeStruct(local_blocks.shape, jnp.bfloat16),
            jax.ShapeDtypeStruct((peers, width, vec_count, block_size), jnp.bfloat16),
        )
        field_specs = [vmem, smem]
    else:
        out_shape = field
        field_specs = [vmem, vmem]
    return pl.pallas_call(
        functools.partial(product_kernel, first),
        out_shape=out_shape,
        in_specs=[smem, smem, vmem, vmem, vmem] + field_specs,
        out_specs=(vmem, vmem, vmem) if first else vmem,
        scratch_shapes=[pltpu.VMEM((row_blocks, vec_count, block_size), jnp.float32)],
        cost_estimate=pl.CostEstimate(
            flops=2 * slots * vec_count * block_size * block_size,
            transcendentals=0,
            bytes_accessed=tiles.size * 2 + ghost_blocks.size * 2 + 3 * field.size * 4,
        ),
    )(pattern_flat, scalars, tiles, local_blocks, ghost_blocks, *fields)


def on_device(
    basis_values, potential, contrib_index, pattern, ghost_list, state, damp_lower, damp_upper
):
    n_rows = lax.axis_size("rows")
    n_cols = lax.axis_size("cols")
    basis_blocks, points, block_size = basis_values.shape
    vec_count = state.shape[0]
    row_blocks = state.shape[1] // block_size
    group_slots = pattern.shape[1]
    slot_count = group_slots // n_cols
    ghost_width = ghost_list.shape[2]

    ghost_ids = ghost_list[0]
    owners = jnp.arange(n_rows, dtype=jnp.int32)[:, None] * row_blocks
    requested = jnp.where(ghost_ids >= 0, ghost_ids - owners, -1)
    target_row = contrib_index[:, 0]
    to_target = target_row[:, None] == jnp.arange(n_rows, dtype=jnp.int32)[None, :]
    slot_for_target = jnp.max(jnp.where(to_target, contrib_index[:, 1:2], -1), axis=0)
    index_send = jnp.concatenate([requested, slot_for_target[:, None]], axis=1)
    index_recv = lax.all_to_all(index_send, "rows", split_axis=0, concat_axis=0, tiled=True)
    wanted_by = index_recv[:, :ghost_width]
    arrived_slots = index_recv[:, ghost_width]

    center = (damp_upper[0] + damp_lower[0]) / 2.0
    half_width = (damp_upper[0] - damp_lower[0]) / 2.0

    def own_blocks(vectors):
        return (
            vectors.astype(jnp.bfloat16)
            .reshape(vec_count, row_blocks, block_size)
            .transpose(1, 0, 2)
        )

    def ghost_payload(blocks):
        return jnp.where(
            (wanted_by >= 0)[:, :, None, None],
            blocks[jnp.clip(wanted_by, 0, row_blocks - 1)],
            jnp.zeros((), jnp.bfloat16),
        )

    def exchange_ghosts(outgoing):
        arrived = lax.all_to_all(outgoing, "rows", split_axis=0, concat_axis=0, tiled=True)
        return arrived.reshape(n_rows * ghost_width, vec_count, block_size)

    state_blocks = own_blocks(state)
    state_outgoing = ghost_payload(state_blocks)

    weighted = (basis_values.astype(jnp.float32) * potential[None, :, None]).astype(jnp.bfloat16)
    send_tiles = presum_tiles(contrib_index.reshape(-1), basis_values, weighted, n_rows)
    arrived_tiles = lax.all_to_all(send_tiles, "rows", split_axis=0, concat_axis=0, tiled=True)
    arrived_tiles, state_outgoing = lax.optimization_barrier((arrived_tiles, state_outgoing))
    state_ghosts = exchange_ghosts(state_outgoing)
    slot_wanted = jnp.arange(slot_count, dtype=jnp.int32)
    selector = (arrived_slots[None, :] == slot_wanted[:, None]).astype(jnp.bfloat16)
    assembled = jnp.dot(
        selector,
        arrived_tiles.reshape(n_rows, block_size * block_size),
        preferred_element_type=jnp.float32,
    )
    assembled = assembled.astype(jnp.bfloat16).reshape(slot_count, block_size, block_size)
    group_tiles = lax.all_gather(assembled, "cols", axis=0, tiled=True)

    pattern_flat = pattern.reshape(-1)
    scalars = jnp.stack([center, half_width])
    first_term, first_blocks, first_outgoing = apply_tiles(
        pattern_flat, scalars, group_tiles, state_blocks, state_ghosts, (state, wanted_by.reshape(-1)), ghost_width
    )
    second_term = apply_tiles(
        pattern_flat,
        scalars,
        group_tiles,
        first_blocks,
        exchange_ghosts(first_outgoing),
        (first_term, state),
        ghost_width,
        first=False,
    )
    return (first_term, second_term)


def solution(mesh):
    in_specs = (
        P(("rows", "cols"), None, None),
        P(("rows", "cols")),
        P(("rows", "cols"), None),
        P("rows", None, None),
        P("rows", None, None),
        P("cols", "rows"),
        P(),
        P(),
    )
    out_specs = (P("cols", "rows"), P("cols", "rows"))
    return jax.shard_map(
        on_device, mesh=mesh, in_specs=in_specs, out_specs=out_specs, check_vma=False
    )
```

```python
import functools

import jax
import jax.numpy as jnp
from jax import lax
from jax.experimental import pallas as pl
from jax.experimental.pallas import tpu as pltpu
from jax.sharding import PartitionSpec as P


def presum_kernel(index_ref, potential_ref, basis_ref, out_ref, stacked_ref, tiles_ref, acc_ref):
    blocks, block_size = basis_ref.shape[0], basis_ref.shape[2]
    for right in range(blocks):
        weighted = basis_ref[right].astype(jnp.float32) * potential_ref[...]
        stacked_ref[right * block_size : (right + 1) * block_size] = weighted.T.astype(jnp.bfloat16)
    for left in range(blocks):
        product = jnp.dot(stacked_ref[...], basis_ref[left], preferred_element_type=jnp.float32)
        for right in range(blocks):
            tiles_ref[left, right] = product[right * block_size : (right + 1) * block_size].astype(
                jnp.bfloat16
            )
    acc_ref[...] = jnp.zeros_like(acc_ref)

    def body(s, carry):
        target = index_ref[4 * s]
        acc_ref[target] += tiles_ref[index_ref[4 * s + 2], index_ref[4 * s + 3]].astype(jnp.float32)
        return carry

    lax.fori_loop(0, index_ref.shape[0] // 4, body, 0, unroll=8)
    out_ref[...] = acc_ref[...].astype(out_ref.dtype)


def presum_tiles(index_flat, basis, potential, n_rows):
    blocks, points, block_size = basis.shape
    return pl.pallas_call(
        presum_kernel,
        out_shape=jax.ShapeDtypeStruct((n_rows, block_size, block_size), jnp.bfloat16),
        in_specs=[
            pl.BlockSpec(memory_space=pltpu.SMEM),
            pl.BlockSpec(memory_space=pltpu.VMEM),
            pl.BlockSpec(memory_space=pltpu.VMEM),
        ],
        out_specs=pl.BlockSpec(memory_space=pltpu.VMEM),
        scratch_shapes=[
            pltpu.VMEM((blocks * block_size, points), jnp.bfloat16),
            pltpu.VMEM((blocks, blocks, block_size, block_size), jnp.bfloat16),
            pltpu.VMEM((n_rows, block_size, block_size), jnp.float32),
        ],
        cost_estimate=pl.CostEstimate(
            flops=2 * blocks * blocks * points * block_size * block_size,
            transcendentals=0,
            bytes_accessed=2 * basis.size * 2 + n_rows * block_size * block_size * 2,
        ),
    )(index_flat, potential[:, None], basis)


def product_kernel(first, pattern_ref, scalar_ref, tiles_ref, local_ref, ghost_ref, *refs):
    row_blocks, vec_count, block_size = local_ref.shape
    acc_ref = refs[-1]
    acc_ref[...] = jnp.zeros_like(acc_ref)

    def body(g, carry):
        row = pattern_ref[2 * g]
        source = pattern_ref[2 * g + 1]
        local = local_ref[jnp.minimum(source, row_blocks - 1)]
        ghost = ghost_ref[jnp.maximum(source - row_blocks, 0)]
        operand = jnp.where(source < row_blocks, local, ghost)
        acc_ref[row] += jnp.dot(operand, tiles_ref[g], preferred_element_type=jnp.float32)
        return carry

    lax.fori_loop(0, tiles_ref.shape[0], body, 0, unroll=8)
    center = scalar_ref[0]
    half_width = scalar_ref[1]
    if first:
        state_ref, wanted_ref, out_ref, blocks_ref, outgoing_ref = refs[:5]
        for row in range(row_blocks):
            lanes = slice(row * block_size, (row + 1) * block_size)
            term = (acc_ref[row] - center * state_ref[:, lanes]) / half_width
            out_ref[:, lanes] = term
            blocks_ref[row] = term.astype(blocks_ref.dtype)
        width = outgoing_ref.shape[1]

        def send(e, carry):
            wanted = wanted_ref[e]
            block = blocks_ref[jnp.clip(wanted, 0, row_blocks - 1)]
            outgoing_ref[e // width, e % width] = jnp.where(wanted >= 0, block, jnp.zeros_like(block))
            return carry

        lax.fori_loop(0, wanted_ref.shape[0], send, 0, unroll=8)
    else:
        first_ref, state_ref, out_ref = refs[0], refs[1], refs[2]
        for row in range(row_blocks):
            lanes = slice(row * block_size, (row + 1) * block_size)
            out_ref[:, lanes] = (
                2.0 * (acc_ref[row] - center * first_ref[:, lanes]) / half_width
                - state_ref[:, lanes]
            )


def apply_tiles(pattern_flat, scalars, tiles, local_blocks, ghost_blocks, fields, width, first=True):
    row_blocks, vec_count, block_size = local_blocks.shape
    slots = tiles.shape[0]
    field = jax.ShapeDtypeStruct((vec_count, row_blocks * block_size), jnp.float32)
    vmem = pl.BlockSpec(memory_space=pltpu.VMEM)
    smem = pl.BlockSpec(memory_space=pltpu.SMEM)
    if first:
        peers = fields[1].shape[0] // width
        out_shape = (
            field,
            jax.ShapeDtypeStruct(local_blocks.shape, jnp.bfloat16),
            jax.ShapeDtypeStruct((peers, width, vec_count, block_size), jnp.bfloat16),
        )
        field_specs = [vmem, smem]
    else:
        out_shape = field
        field_specs = [vmem, vmem]
    return pl.pallas_call(
        functools.partial(product_kernel, first),
        out_shape=out_shape,
        in_specs=[smem, smem, vmem, vmem, vmem] + field_specs,
        out_specs=(vmem, vmem, vmem) if first else vmem,
        scratch_shapes=[pltpu.VMEM((row_blocks, vec_count, block_size), jnp.float32)],
        cost_estimate=pl.CostEstimate(
            flops=2 * slots * vec_count * block_size * block_size,
            transcendentals=0,
            bytes_accessed=tiles.size * 2 + ghost_blocks.size * 2 + 3 * field.size * 4,
        ),
    )(pattern_flat, scalars, tiles, local_blocks, ghost_blocks, *fields)


def on_device(
    basis_values, potential, contrib_index, pattern, ghost_list, state, damp_lower, damp_upper
):
    n_rows = lax.axis_size("rows")
    n_cols = lax.axis_size("cols")
    basis_blocks, points, block_size = basis_values.shape
    vec_count = state.shape[0]
    row_blocks = state.shape[1] // block_size
    group_slots = pattern.shape[1]
    slot_count = group_slots // n_cols
    ghost_width = ghost_list.shape[2]

    ghost_ids = ghost_list[0]
    owners = jnp.arange(n_rows, dtype=jnp.int32)[:, None] * row_blocks
    requested = jnp.where(ghost_ids >= 0, ghost_ids - owners, -1)
    target_row = contrib_index[:, 0]
    to_target = target_row[:, None] == jnp.arange(n_rows, dtype=jnp.int32)[None, :]
    slot_for_target = jnp.max(jnp.where(to_target, contrib_index[:, 1:2], -1), axis=0)
    index_send = jnp.concatenate([requested, slot_for_target[:, None]], axis=1)
    index_recv = lax.all_to_all(index_send, "rows", split_axis=0, concat_axis=0, tiled=True)
    wanted_by = index_recv[:, :ghost_width]
    arrived_slots = index_recv[:, ghost_width]

    center = (damp_upper[0] + damp_lower[0]) / 2.0
    half_width = (damp_upper[0] - damp_lower[0]) / 2.0

    def own_blocks(vectors):
        return (
            vectors.astype(jnp.bfloat16)
            .reshape(vec_count, row_blocks, block_size)
            .transpose(1, 0, 2)
        )

    def ghost_payload(blocks):
        return jnp.where(
            (wanted_by >= 0)[:, :, None, None],
            blocks[jnp.clip(wanted_by, 0, row_blocks - 1)],
            jnp.zeros((), jnp.bfloat16),
        )

    def exchange_ghosts(outgoing):
        arrived = lax.all_to_all(outgoing, "rows", split_axis=0, concat_axis=0, tiled=True)
        return arrived.reshape(n_rows * ghost_width, vec_count, block_size)

    state_blocks = own_blocks(state)
    state_outgoing = ghost_payload(state_blocks)

    send_tiles = presum_tiles(contrib_index.reshape(-1), basis_values, potential, n_rows)
    arrived_tiles = lax.all_to_all(send_tiles, "rows", split_axis=0, concat_axis=0, tiled=True)
    arrived_tiles, state_outgoing = lax.optimization_barrier((arrived_tiles, state_outgoing))
    state_ghosts = exchange_ghosts(state_outgoing)
    slot_wanted = jnp.arange(slot_count, dtype=jnp.int32)
    selector = (arrived_slots[None, :] == slot_wanted[:, None]).astype(jnp.bfloat16)
    assembled = jnp.dot(
        selector,
        arrived_tiles.reshape(n_rows, block_size * block_size),
        preferred_element_type=jnp.float32,
    )
    assembled = assembled.astype(jnp.bfloat16).reshape(slot_count, block_size, block_size)
    group_tiles = lax.all_gather(assembled, "cols", axis=0, tiled=True)

    pattern_flat = pattern.reshape(-1)
    scalars = jnp.stack([center, half_width])
    first_term, first_blocks, first_outgoing = apply_tiles(
        pattern_flat, scalars, group_tiles, state_blocks, state_ghosts, (state, wanted_by.reshape(-1)), ghost_width
    )
    second_term = apply_tiles(
        pattern_flat,
        scalars,
        group_tiles,
        first_blocks,
        exchange_ghosts(first_outgoing),
        (first_term, state),
        ghost_width,
        first=False,
    )
    return (first_term, second_term)


def solution(mesh):
    in_specs = (
        P(("rows", "cols"), None, None),
        P(("rows", "cols")),
        P(("rows", "cols"), None),
        P("rows", None, None),
        P("rows", None, None),
        P("cols", "rows"),
        P(),
        P(),
    )
    out_specs = (P("cols", "rows"), P("cols", "rows"))
    return jax.shard_map(
        on_device, mesh=mesh, in_specs=in_specs, out_specs=out_specs, check_vma=False
    )
```

```python
import functools

import jax
import jax.numpy as jnp
from jax import lax
from jax.experimental import pallas as pl
from jax.experimental.pallas import tpu as pltpu
from jax.sharding import PartitionSpec as P


def presum_kernel(index_ref, potential_ref, basis_ref, out_ref, stacked_ref, tiles_ref, acc_ref):
    blocks, block_size = basis_ref.shape[0], basis_ref.shape[2]
    for right in range(blocks):
        weighted = basis_ref[right].astype(jnp.float32).T * potential_ref[...]
        stacked_ref[right * block_size : (right + 1) * block_size] = weighted.astype(jnp.bfloat16)
    for left in range(blocks):
        product = jnp.dot(stacked_ref[...], basis_ref[left], preferred_element_type=jnp.float32)
        for right in range(blocks):
            tiles_ref[left, right] = product[right * block_size : (right + 1) * block_size].astype(
                jnp.bfloat16
            )
    acc_ref[...] = jnp.zeros_like(acc_ref)

    def body(s, carry):
        target = index_ref[4 * s]
        acc_ref[target] += tiles_ref[index_ref[4 * s + 2], index_ref[4 * s + 3]].astype(jnp.float32)
        return carry

    lax.fori_loop(0, index_ref.shape[0] // 4, body, 0, unroll=8)
    out_ref[...] = acc_ref[...].astype(out_ref.dtype)


def presum_tiles(index_flat, basis, potential, n_rows):
    blocks, points, block_size = basis.shape
    return pl.pallas_call(
        presum_kernel,
        out_shape=jax.ShapeDtypeStruct((n_rows, block_size, block_size), jnp.bfloat16),
        in_specs=[
            pl.BlockSpec(memory_space=pltpu.SMEM),
            pl.BlockSpec(memory_space=pltpu.VMEM),
            pl.BlockSpec(memory_space=pltpu.VMEM),
        ],
        out_specs=pl.BlockSpec(memory_space=pltpu.VMEM),
        scratch_shapes=[
            pltpu.VMEM((blocks * block_size, points), jnp.bfloat16),
            pltpu.VMEM((blocks, blocks, block_size, block_size), jnp.bfloat16),
            pltpu.VMEM((n_rows, block_size, block_size), jnp.float32),
        ],
        cost_estimate=pl.CostEstimate(
            flops=2 * blocks * blocks * points * block_size * block_size,
            transcendentals=0,
            bytes_accessed=2 * basis.size * 2 + n_rows * block_size * block_size * 2,
        ),
    )(index_flat, potential[None, :], basis)


def product_kernel(first, pattern_ref, scalar_ref, tiles_ref, local_ref, ghost_ref, *refs):
    row_blocks, vec_count, block_size = local_ref.shape
    acc_ref = refs[-1]
    acc_ref[...] = jnp.zeros_like(acc_ref)

    def body(g, carry):
        row = pattern_ref[2 * g]
        source = pattern_ref[2 * g + 1]
        local = local_ref[jnp.minimum(source, row_blocks - 1)]
        ghost = ghost_ref[jnp.maximum(source - row_blocks, 0)]
        operand = jnp.where(source < row_blocks, local, ghost)
        acc_ref[row] += jnp.dot(operand, tiles_ref[g], preferred_element_type=jnp.float32)
        return carry

    lax.fori_loop(0, tiles_ref.shape[0], body, 0, unroll=8)
    center = scalar_ref[0]
    half_width = scalar_ref[1]
    if first:
        state_ref, wanted_ref, out_ref, blocks_ref, outgoing_ref = refs[:5]
        for row in range(row_blocks):
            lanes = slice(row * block_size, (row + 1) * block_size)
            term = (acc_ref[row] - center * state_ref[:, lanes]) / half_width
            out_ref[:, lanes] = term
            blocks_ref[row] = term.astype(blocks_ref.dtype)
        width = outgoing_ref.shape[1]

        def send(e, carry):
            wanted = wanted_ref[e]
            block = blocks_ref[jnp.clip(wanted, 0, row_blocks - 1)]
            outgoing_ref[e // width, e % width] = jnp.where(wanted >= 0, block, jnp.zeros_like(block))
            return carry

        lax.fori_loop(0, wanted_ref.shape[0], send, 0, unroll=8)
    else:
        first_ref, state_ref, out_ref = refs[0], refs[1], refs[2]
        for row in range(row_blocks):
            lanes = slice(row * block_size, (row + 1) * block_size)
            out_ref[:, lanes] = (
                2.0 * (acc_ref[row] - center * first_ref[:, lanes]) / half_width
                - state_ref[:, lanes]
            )


def apply_tiles(pattern_flat, scalars, tiles, local_blocks, ghost_blocks, fields, width, first=True):
    row_blocks, vec_count, block_size = local_blocks.shape
    slots = tiles.shape[0]
    field = jax.ShapeDtypeStruct((vec_count, row_blocks * block_size), jnp.float32)
    vmem = pl.BlockSpec(memory_space=pltpu.VMEM)
    smem = pl.BlockSpec(memory_space=pltpu.SMEM)
    if first:
        peers = fields[1].shape[0] // width
        out_shape = (
            field,
            jax.ShapeDtypeStruct(local_blocks.shape, jnp.bfloat16),
            jax.ShapeDtypeStruct((peers, width, vec_count, block_size), jnp.bfloat16),
        )
        field_specs = [vmem, smem]
    else:
        out_shape = field
        field_specs = [vmem, vmem]
    return pl.pallas_call(
        functools.partial(product_kernel, first),
        out_shape=out_shape,
        in_specs=[smem, smem, vmem, vmem, vmem] + field_specs,
        out_specs=(vmem, vmem, vmem) if first else vmem,
        scratch_shapes=[pltpu.VMEM((row_blocks, vec_count, block_size), jnp.float32)],
        cost_estimate=pl.CostEstimate(
            flops=2 * slots * vec_count * block_size * block_size,
            transcendentals=0,
            bytes_accessed=tiles.size * 2 + ghost_blocks.size * 2 + 3 * field.size * 4,
        ),
    )(pattern_flat, scalars, tiles, local_blocks, ghost_blocks, *fields)


def on_device(
    basis_values, potential, contrib_index, pattern, ghost_list, state, damp_lower, damp_upper
):
    n_rows = lax.axis_size("rows")
    n_cols = lax.axis_size("cols")
    basis_blocks, points, block_size = basis_values.shape
    vec_count = state.shape[0]
    row_blocks = state.shape[1] // block_size
    group_slots = pattern.shape[1]
    slot_count = group_slots // n_cols
    ghost_width = ghost_list.shape[2]

    ghost_ids = ghost_list[0]
    owners = jnp.arange(n_rows, dtype=jnp.int32)[:, None] * row_blocks
    requested = jnp.where(ghost_ids >= 0, ghost_ids - owners, -1)
    target_row = contrib_index[:, 0]
    to_target = target_row[:, None] == jnp.arange(n_rows, dtype=jnp.int32)[None, :]
    slot_for_target = jnp.max(jnp.where(to_target, contrib_index[:, 1:2], -1), axis=0)
    index_send = jnp.concatenate([requested, slot_for_target[:, None]], axis=1)
    index_recv = lax.all_to_all(index_send, "rows", split_axis=0, concat_axis=0, tiled=True)
    wanted_by = index_recv[:, :ghost_width]
    arrived_slots = index_recv[:, ghost_width]

    center = (damp_upper[0] + damp_lower[0]) / 2.0
    half_width = (damp_upper[0] - damp_lower[0]) / 2.0

    def own_blocks(vectors):
        return (
            vectors.astype(jnp.bfloat16)
            .reshape(vec_count, row_blocks, block_size)
            .transpose(1, 0, 2)
        )

    def ghost_payload(blocks):
        return jnp.where(
            (wanted_by >= 0)[:, :, None, None],
            blocks[jnp.clip(wanted_by, 0, row_blocks - 1)],
            jnp.zeros((), jnp.bfloat16),
        )

    def exchange_ghosts(outgoing):
        arrived = lax.all_to_all(outgoing, "rows", split_axis=0, concat_axis=0, tiled=True)
        return arrived.reshape(n_rows * ghost_width, vec_count, block_size)

    state_blocks = own_blocks(state)
    state_outgoing = ghost_payload(state_blocks)

    send_tiles = presum_tiles(contrib_index.reshape(-1), basis_values, potential, n_rows)
    arrived_tiles = lax.all_to_all(send_tiles, "rows", split_axis=0, concat_axis=0, tiled=True)
    arrived_tiles, state_outgoing = lax.optimization_barrier((arrived_tiles, state_outgoing))
    state_ghosts = exchange_ghosts(state_outgoing)
    slot_wanted = jnp.arange(slot_count, dtype=jnp.int32)
    selector = (arrived_slots[None, :] == slot_wanted[:, None]).astype(jnp.bfloat16)
    assembled = jnp.dot(
        selector,
        arrived_tiles.reshape(n_rows, block_size * block_size),
        preferred_element_type=jnp.float32,
    )
    assembled = assembled.astype(jnp.bfloat16).reshape(slot_count, block_size, block_size)
    group_tiles = lax.all_gather(assembled, "cols", axis=0, tiled=True)

    pattern_flat = pattern.reshape(-1)
    scalars = jnp.stack([center, half_width])
    first_term, first_blocks, first_outgoing = apply_tiles(
        pattern_flat, scalars, group_tiles, state_blocks, state_ghosts, (state, wanted_by.reshape(-1)), ghost_width
    )
    second_term = apply_tiles(
        pattern_flat,
        scalars,
        group_tiles,
        first_blocks,
        exchange_ghosts(first_outgoing),
        (first_term, state),
        ghost_width,
        first=False,
    )
    return (first_term, second_term)


def solution(mesh):
    in_specs = (
        P(("rows", "cols"), None, None),
        P(("rows", "cols")),
        P(("rows", "cols"), None),
        P("rows", None, None),
        P("rows", None, None),
        P("cols", "rows"),
        P(),
        P(),
    )
    out_specs = (P("cols", "rows"), P("cols", "rows"))
    return jax.shard_map(
        on_device, mesh=mesh, in_specs=in_specs, out_specs=out_specs, check_vma=False
    )
```

```python
import functools

import jax
import jax.numpy as jnp
from jax import lax
from jax.experimental import pallas as pl
from jax.experimental.pallas import tpu as pltpu
from jax.sharding import PartitionSpec as P


def presum_kernel(index_ref, potential_ref, basis_ref, out_ref, stacked_ref, tiles_ref, acc_ref):
    blocks, block_size = basis_ref.shape[0], basis_ref.shape[2]
    for right in range(blocks):
        weighted = basis_ref[right].astype(jnp.float32).T * potential_ref[...]
        stacked_ref[right * block_size : (right + 1) * block_size] = weighted.astype(jnp.bfloat16)
    for left in range(blocks):
        product = jnp.dot(stacked_ref[...], basis_ref[left], preferred_element_type=jnp.float32)
        for right in range(blocks):
            tiles_ref[left, right] = product[right * block_size : (right + 1) * block_size].astype(
                jnp.bfloat16
            )
    acc_ref[...] = jnp.zeros_like(acc_ref)

    def body(s, carry):
        target = index_ref[s, 0]
        acc_ref[target] += tiles_ref[index_ref[s, 2], index_ref[s, 3]].astype(jnp.float32)
        return carry

    lax.fori_loop(0, index_ref.shape[0], body, 0, unroll=8)
    out_ref[...] = acc_ref[...].astype(out_ref.dtype)


def presum_tiles(index, basis, potential, n_rows):
    blocks, points, block_size = basis.shape
    return pl.pallas_call(
        presum_kernel,
        out_shape=jax.ShapeDtypeStruct((n_rows, block_size, block_size), jnp.bfloat16),
        in_specs=[
            pl.BlockSpec(memory_space=pltpu.SMEM),
            pl.BlockSpec(memory_space=pltpu.VMEM),
            pl.BlockSpec(memory_space=pltpu.VMEM),
        ],
        out_specs=pl.BlockSpec(memory_space=pltpu.VMEM),
        scratch_shapes=[
            pltpu.VMEM((blocks * block_size, points), jnp.bfloat16),
            pltpu.VMEM((blocks, blocks, block_size, block_size), jnp.bfloat16),
            pltpu.VMEM((n_rows, block_size, block_size), jnp.float32),
        ],
        cost_estimate=pl.CostEstimate(
            flops=2 * blocks * blocks * points * block_size * block_size,
            transcendentals=0,
            bytes_accessed=2 * basis.size * 2 + n_rows * block_size * block_size * 2,
        ),
    )(index, potential[None, :], basis)


def product_kernel(first, pattern_ref, scalar_ref, tiles_ref, local_ref, ghost_ref, *refs):
    row_blocks, vec_count, block_size = local_ref.shape
    acc_ref = refs[-1]
    acc_ref[...] = jnp.zeros_like(acc_ref)

    def body(g, carry):
        row = pattern_ref[2 * g]
        source = pattern_ref[2 * g + 1]
        local = local_ref[jnp.minimum(source, row_blocks - 1)]
        ghost = ghost_ref[jnp.maximum(source - row_blocks, 0)]
        operand = jnp.where(source < row_blocks, local, ghost)
        acc_ref[row] += jnp.dot(operand, tiles_ref[g], preferred_element_type=jnp.float32)
        return carry

    lax.fori_loop(0, tiles_ref.shape[0], body, 0, unroll=8)
    center = scalar_ref[0]
    half_width = scalar_ref[1]
    if first:
        state_ref, wanted_ref, out_ref, blocks_ref, outgoing_ref = refs[:5]
        for row in range(row_blocks):
            lanes = slice(row * block_size, (row + 1) * block_size)
            term = (acc_ref[row] - center * state_ref[:, lanes]) / half_width
            out_ref[:, lanes] = term
            blocks_ref[row] = term.astype(blocks_ref.dtype)
        width = outgoing_ref.shape[1]

        def send(e, carry):
            wanted = wanted_ref[e]
            block = blocks_ref[jnp.clip(wanted, 0, row_blocks - 1)]
            outgoing_ref[e // width, e % width] = jnp.where(wanted >= 0, block, jnp.zeros_like(block))
            return carry

        lax.fori_loop(0, wanted_ref.shape[0], send, 0, unroll=8)
    else:
        first_ref, state_ref, out_ref = refs[0], refs[1], refs[2]
        for row in range(row_blocks):
            lanes = slice(row * block_size, (row + 1) * block_size)
            out_ref[:, lanes] = (
                2.0 * (acc_ref[row] - center * first_ref[:, lanes]) / half_width
                - state_ref[:, lanes]
            )


def apply_tiles(pattern_flat, scalars, tiles, local_blocks, ghost_blocks, fields, width, first=True):
    row_blocks, vec_count, block_size = local_blocks.shape
    slots = tiles.shape[0]
    field = jax.ShapeDtypeStruct((vec_count, row_blocks * block_size), jnp.float32)
    vmem = pl.BlockSpec(memory_space=pltpu.VMEM)
    smem = pl.BlockSpec(memory_space=pltpu.SMEM)
    if first:
        peers = fields[1].shape[0] // width
        out_shape = (
            field,
            jax.ShapeDtypeStruct(local_blocks.shape, jnp.bfloat16),
            jax.ShapeDtypeStruct((peers, width, vec_count, block_size), jnp.bfloat16),
        )
        field_specs = [vmem, smem]
    else:
        out_shape = field
        field_specs = [vmem, vmem]
    return pl.pallas_call(
        functools.partial(product_kernel, first),
        out_shape=out_shape,
        in_specs=[smem, smem, vmem, vmem, vmem] + field_specs,
        out_specs=(vmem, vmem, vmem) if first else vmem,
        scratch_shapes=[pltpu.VMEM((row_blocks, vec_count, block_size), jnp.float32)],
        cost_estimate=pl.CostEstimate(
            flops=2 * slots * vec_count * block_size * block_size,
            transcendentals=0,
            bytes_accessed=tiles.size * 2 + ghost_blocks.size * 2 + 3 * field.size * 4,
        ),
    )(pattern_flat, scalars, tiles, local_blocks, ghost_blocks, *fields)


def on_device(
    basis_values, potential, contrib_index, pattern, ghost_list, state, damp_lower, damp_upper
):
    n_rows = lax.axis_size("rows")
    n_cols = lax.axis_size("cols")
    basis_blocks, points, block_size = basis_values.shape
    vec_count = state.shape[0]
    row_blocks = state.shape[1] // block_size
    group_slots = pattern.shape[1]
    slot_count = group_slots // n_cols
    ghost_width = ghost_list.shape[2]

    ghost_ids = ghost_list[0]
    owners = jnp.arange(n_rows, dtype=jnp.int32)[:, None] * row_blocks
    requested = jnp.where(ghost_ids >= 0, ghost_ids - owners, -1)
    target_row = contrib_index[:, 0]
    to_target = target_row[:, None] == jnp.arange(n_rows, dtype=jnp.int32)[None, :]
    slot_for_target = jnp.max(jnp.where(to_target, contrib_index[:, 1:2], -1), axis=0)
    index_send = jnp.concatenate([requested, slot_for_target[:, None]], axis=1)
    index_recv = lax.all_to_all(index_send, "rows", split_axis=0, concat_axis=0, tiled=True)
    wanted_by = index_recv[:, :ghost_width]
    arrived_slots = index_recv[:, ghost_width]

    center = (damp_upper[0] + damp_lower[0]) / 2.0
    half_width = (damp_upper[0] - damp_lower[0]) / 2.0

    def own_blocks(vectors):
        return (
            vectors.astype(jnp.bfloat16)
            .reshape(vec_count, row_blocks, block_size)
            .transpose(1, 0, 2)
        )

    def ghost_payload(blocks):
        return jnp.where(
            (wanted_by >= 0)[:, :, None, None],
            blocks[jnp.clip(wanted_by, 0, row_blocks - 1)],
            jnp.zeros((), jnp.bfloat16),
        )

    def exchange_ghosts(outgoing):
        arrived = lax.all_to_all(outgoing, "rows", split_axis=0, concat_axis=0, tiled=True)
        return arrived.reshape(n_rows * ghost_width, vec_count, block_size)

    state_blocks = own_blocks(state)
    state_outgoing = ghost_payload(state_blocks)

    send_tiles = presum_tiles(contrib_index, basis_values, potential, n_rows)
    arrived_tiles = lax.all_to_all(send_tiles, "rows", split_axis=0, concat_axis=0, tiled=True)
    arrived_tiles, state_outgoing = lax.optimization_barrier((arrived_tiles, state_outgoing))
    state_ghosts = exchange_ghosts(state_outgoing)
    slot_wanted = jnp.arange(slot_count, dtype=jnp.int32)
    selector = (arrived_slots[None, :] == slot_wanted[:, None]).astype(jnp.bfloat16)
    assembled = jnp.dot(
        selector,
        arrived_tiles.reshape(n_rows, block_size * block_size),
        preferred_element_type=jnp.float32,
    )
    assembled = assembled.astype(jnp.bfloat16).reshape(slot_count, block_size, block_size)
    group_tiles = lax.all_gather(assembled, "cols", axis=0, tiled=True)

    pattern_flat = pattern.reshape(-1)
    scalars = jnp.stack([center, half_width])
    first_term, first_blocks, first_outgoing = apply_tiles(
        pattern_flat, scalars, group_tiles, state_blocks, state_ghosts, (state, wanted_by.reshape(-1)), ghost_width
    )
    second_term = apply_tiles(
        pattern_flat,
        scalars,
        group_tiles,
        first_blocks,
        exchange_ghosts(first_outgoing),
        (first_term, state),
        ghost_width,
        first=False,
    )
    return (first_term, second_term)


def solution(mesh):
    in_specs = (
        P(("rows", "cols"), None, None),
        P(("rows", "cols")),
        P(("rows", "cols"), None),
        P("rows", None, None),
        P("rows", None, None),
        P("cols", "rows"),
        P(),
        P(),
    )
    out_specs = (P("cols", "rows"), P("cols", "rows"))
    return jax.shard_map(
        on_device, mesh=mesh, in_specs=in_specs, out_specs=out_specs, check_vma=False
    )
```

```python
import functools

import jax
import jax.numpy as jnp
from jax import lax
from jax.experimental import pallas as pl
from jax.experimental.pallas import tpu as pltpu
from jax.sharding import PartitionSpec as P


def presum_kernel(index_ref, potential_ref, basis_ref, out_ref, stacked_ref, tiles_ref, acc_ref):
    blocks, block_size = basis_ref.shape[0], basis_ref.shape[2]
    for right in range(blocks):
        weighted = basis_ref[right].astype(jnp.float32).T * potential_ref[...]
        stacked_ref[right * block_size : (right + 1) * block_size] = weighted.astype(jnp.bfloat16)
    for left in range(blocks):
        product = jnp.dot(stacked_ref[...], basis_ref[left], preferred_element_type=jnp.float32)
        for right in range(blocks):
            tiles_ref[left, right] = product[right * block_size : (right + 1) * block_size].astype(
                jnp.bfloat16
            )
    acc_ref[...] = jnp.zeros_like(acc_ref)

    def body(s, carry):
        target = index_ref[4 * s]
        acc_ref[target] += tiles_ref[index_ref[4 * s + 2], index_ref[4 * s + 3]].astype(jnp.float32)
        return carry

    lax.fori_loop(0, index_ref.shape[0] // 4, body, 0, unroll=8)
    out_ref[...] = acc_ref[...].astype(out_ref.dtype)


def presum_tiles(index_flat, basis, potential, n_rows):
    blocks, points, block_size = basis.shape
    return pl.pallas_call(
        presum_kernel,
        out_shape=jax.ShapeDtypeStruct((n_rows, block_size, block_size), jnp.bfloat16),
        in_specs=[
            pl.BlockSpec(memory_space=pltpu.SMEM),
            pl.BlockSpec(memory_space=pltpu.VMEM),
            pl.BlockSpec(memory_space=pltpu.VMEM),
        ],
        out_specs=pl.BlockSpec(memory_space=pltpu.VMEM),
        scratch_shapes=[
            pltpu.VMEM((blocks * block_size, points), jnp.bfloat16),
            pltpu.VMEM((blocks, blocks, block_size, block_size), jnp.bfloat16),
            pltpu.VMEM((n_rows, block_size, block_size), jnp.float32),
        ],
        compiler_params=pltpu.CompilerParams(vmem_limit_bytes=24 * 1024 * 1024),
        cost_estimate=pl.CostEstimate(
            flops=2 * blocks * blocks * points * block_size * block_size,
            transcendentals=0,
            bytes_accessed=2 * basis.size * 2 + n_rows * block_size * block_size * 2,
        ),
    )(index_flat, potential[None, :], basis)


def product_kernel(first, pattern_ref, scalar_ref, tiles_ref, local_ref, ghost_ref, *refs):
    row_blocks, vec_count, block_size = local_ref.shape
    acc_ref = refs[-1]
    acc_ref[...] = jnp.zeros_like(acc_ref)

    def body(g, carry):
        row = pattern_ref[2 * g]
        source = pattern_ref[2 * g + 1]
        local = local_ref[jnp.minimum(source, row_blocks - 1)]
        ghost = ghost_ref[jnp.maximum(source - row_blocks, 0)]
        operand = jnp.where(source < row_blocks, local, ghost)
        acc_ref[row] += jnp.dot(operand, tiles_ref[g], preferred_element_type=jnp.float32)
        return carry

    lax.fori_loop(0, tiles_ref.shape[0], body, 0, unroll=8)
    center = scalar_ref[0]
    half_width = scalar_ref[1]
    if first:
        state_ref, wanted_ref, out_ref, blocks_ref, outgoing_ref = refs[:5]
        for row in range(row_blocks):
            lanes = slice(row * block_size, (row + 1) * block_size)
            term = (acc_ref[row] - center * state_ref[:, lanes]) / half_width
            out_ref[:, lanes] = term
            blocks_ref[row] = term.astype(blocks_ref.dtype)
        width = outgoing_ref.shape[1]

        def send(e, carry):
            wanted = wanted_ref[e]
            block = blocks_ref[jnp.clip(wanted, 0, row_blocks - 1)]
            outgoing_ref[e // width, e % width] = jnp.where(wanted >= 0, block, jnp.zeros_like(block))
            return carry

        lax.fori_loop(0, wanted_ref.shape[0], send, 0, unroll=8)
    else:
        first_ref, state_ref, out_ref = refs[0], refs[1], refs[2]
        for row in range(row_blocks):
            lanes = slice(row * block_size, (row + 1) * block_size)
            out_ref[:, lanes] = (
                2.0 * (acc_ref[row] - center * first_ref[:, lanes]) / half_width
                - state_ref[:, lanes]
            )


def apply_tiles(pattern_flat, scalars, tiles, local_blocks, ghost_blocks, fields, width, first=True):
    row_blocks, vec_count, block_size = local_blocks.shape
    slots = tiles.shape[0]
    field = jax.ShapeDtypeStruct((vec_count, row_blocks * block_size), jnp.float32)
    vmem = pl.BlockSpec(memory_space=pltpu.VMEM)
    smem = pl.BlockSpec(memory_space=pltpu.SMEM)
    if first:
        peers = fields[1].shape[0] // width
        out_shape = (
            field,
            jax.ShapeDtypeStruct(local_blocks.shape, jnp.bfloat16),
            jax.ShapeDtypeStruct((peers, width, vec_count, block_size), jnp.bfloat16),
        )
        field_specs = [vmem, smem]
    else:
        out_shape = field
        field_specs = [vmem, vmem]
    return pl.pallas_call(
        functools.partial(product_kernel, first),
        out_shape=out_shape,
        in_specs=[smem, smem, vmem, vmem, vmem] + field_specs,
        out_specs=(vmem, vmem, vmem) if first else vmem,
        scratch_shapes=[pltpu.VMEM((row_blocks, vec_count, block_size), jnp.float32)],
        compiler_params=pltpu.CompilerParams(vmem_limit_bytes=16 * 1024 * 1024),
        cost_estimate=pl.CostEstimate(
            flops=2 * slots * vec_count * block_size * block_size,
            transcendentals=0,
            bytes_accessed=tiles.size * 2 + ghost_blocks.size * 2 + 3 * field.size * 4,
        ),
    )(pattern_flat, scalars, tiles, local_blocks, ghost_blocks, *fields)


def on_device(
    basis_values, potential, contrib_index, pattern, ghost_list, state, damp_lower, damp_upper
):
    n_rows = lax.axis_size("rows")
    n_cols = lax.axis_size("cols")
    basis_blocks, points, block_size = basis_values.shape
    vec_count = state.shape[0]
    row_blocks = state.shape[1] // block_size
    group_slots = pattern.shape[1]
    slot_count = group_slots // n_cols
    ghost_width = ghost_list.shape[2]

    ghost_ids = ghost_list[0]
    owners = jnp.arange(n_rows, dtype=jnp.int32)[:, None] * row_blocks
    requested = jnp.where(ghost_ids >= 0, ghost_ids - owners, -1)
    target_row = contrib_index[:, 0]
    to_target = target_row[:, None] == jnp.arange(n_rows, dtype=jnp.int32)[None, :]
    slot_for_target = jnp.max(jnp.where(to_target, contrib_index[:, 1:2], -1), axis=0)
    index_send = jnp.concatenate([requested, slot_for_target[:, None]], axis=1)
    index_recv = lax.all_to_all(index_send, "rows", split_axis=0, concat_axis=0, tiled=True)
    wanted_by = index_recv[:, :ghost_width]
    arrived_slots = index_recv[:, ghost_width]

    center = (damp_upper[0] + damp_lower[0]) / 2.0
    half_width = (damp_upper[0] - damp_lower[0]) / 2.0

    def own_blocks(vectors):
        return (
            vectors.astype(jnp.bfloat16)
            .reshape(vec_count, row_blocks, block_size)
            .transpose(1, 0, 2)
        )

    def ghost_payload(blocks):
        return jnp.where(
            (wanted_by >= 0)[:, :, None, None],
            blocks[jnp.clip(wanted_by, 0, row_blocks - 1)],
            jnp.zeros((), jnp.bfloat16),
        )

    def exchange_ghosts(outgoing):
        arrived = lax.all_to_all(outgoing, "rows", split_axis=0, concat_axis=0, tiled=True)
        return arrived.reshape(n_rows * ghost_width, vec_count, block_size)

    state_blocks = own_blocks(state)
    state_outgoing = ghost_payload(state_blocks)

    send_tiles = presum_tiles(contrib_index.reshape(-1), basis_values, potential, n_rows)
    arrived_tiles = lax.all_to_all(send_tiles, "rows", split_axis=0, concat_axis=0, tiled=True)
    arrived_tiles, state_outgoing = lax.optimization_barrier((arrived_tiles, state_outgoing))
    state_ghosts = exchange_ghosts(state_outgoing)
    slot_wanted = jnp.arange(slot_count, dtype=jnp.int32)
    selector = (arrived_slots[None, :] == slot_wanted[:, None]).astype(jnp.bfloat16)
    assembled = jnp.dot(
        selector,
        arrived_tiles.reshape(n_rows, block_size * block_size),
        preferred_element_type=jnp.float32,
    )
    assembled = assembled.astype(jnp.bfloat16).reshape(slot_count, block_size, block_size)
    group_tiles = lax.all_gather(assembled, "cols", axis=0, tiled=True)

    pattern_flat = pattern.reshape(-1)
    scalars = jnp.stack([center, half_width])
    first_term, first_blocks, first_outgoing = apply_tiles(
        pattern_flat, scalars, group_tiles, state_blocks, state_ghosts, (state, wanted_by.reshape(-1)), ghost_width
    )
    second_term = apply_tiles(
        pattern_flat,
        scalars,
        group_tiles,
        first_blocks,
        exchange_ghosts(first_outgoing),
        (first_term, state),
        ghost_width,
        first=False,
    )
    return (first_term, second_term)


def solution(mesh):
    in_specs = (
        P(("rows", "cols"), None, None),
        P(("rows", "cols")),
        P(("rows", "cols"), None),
        P("rows", None, None),
        P("rows", None, None),
        P("cols", "rows"),
        P(),
        P(),
    )
    out_specs = (P("cols", "rows"), P("cols", "rows"))
    return jax.shard_map(
        on_device, mesh=mesh, in_specs=in_specs, out_specs=out_specs, check_vma=False
    )
```

```python
import functools

import jax
import jax.numpy as jnp
from jax import lax
from jax.experimental import pallas as pl
from jax.experimental.pallas import tpu as pltpu
from jax.sharding import PartitionSpec as P


def presum_kernel(index_ref, potential_ref, basis_ref, out_ref, stacked_ref, tiles_ref, acc_ref):
    blocks, block_size = basis_ref.shape[0], basis_ref.shape[2]
    for right in range(blocks):
        weighted = basis_ref[right].astype(jnp.float32).T * potential_ref[...]
        stacked_ref[right * block_size : (right + 1) * block_size] = weighted.astype(jnp.bfloat16)
    for left in range(blocks):
        product = jnp.dot(stacked_ref[...], basis_ref[left], preferred_element_type=jnp.float32)
        for right in range(blocks):
            tiles_ref[left, right] = product[right * block_size : (right + 1) * block_size].astype(
                jnp.bfloat16
            )
    acc_ref[...] = jnp.zeros_like(acc_ref)

    def body(s, carry):
        target = index_ref[4 * s]
        acc_ref[target] += tiles_ref[index_ref[4 * s + 2], index_ref[4 * s + 3]].astype(jnp.float32)
        return carry

    lax.fori_loop(0, index_ref.shape[0] // 4, body, 0, unroll=8)
    out_ref[...] = acc_ref[...].astype(out_ref.dtype)


def presum_tiles(index_flat, basis, potential, n_rows):
    blocks, points, block_size = basis.shape
    return pl.pallas_call(
        presum_kernel,
        out_shape=jax.ShapeDtypeStruct((n_rows, block_size, block_size), jnp.bfloat16),
        in_specs=[
            pl.BlockSpec(memory_space=pltpu.SMEM),
            pl.BlockSpec(memory_space=pltpu.VMEM),
            pl.BlockSpec(memory_space=pltpu.VMEM),
        ],
        out_specs=pl.BlockSpec(memory_space=pltpu.VMEM),
        scratch_shapes=[
            pltpu.VMEM((blocks * block_size, points), jnp.bfloat16),
            pltpu.VMEM((blocks, blocks, block_size, block_size), jnp.bfloat16),
            pltpu.VMEM((n_rows, block_size, block_size), jnp.float32),
        ],
        compiler_params=pltpu.CompilerParams(vmem_limit_bytes=24 * 1024 * 1024),
        cost_estimate=pl.CostEstimate(
            flops=2 * blocks * blocks * points * block_size * block_size,
            transcendentals=0,
            bytes_accessed=2 * basis.size * 2 + n_rows * block_size * block_size * 2,
        ),
    )(index_flat, potential[None, :], basis)


def product_kernel(first, pattern_ref, scalar_ref, tiles_ref, local_ref, ghost_ref, *refs):
    row_blocks, vec_count, block_size = local_ref.shape
    acc_ref = refs[-1]
    acc_ref[...] = jnp.zeros_like(acc_ref)

    def body(g, carry):
        row = pattern_ref[2 * g]
        source = pattern_ref[2 * g + 1]
        local = local_ref[jnp.minimum(source, row_blocks - 1)]
        ghost = ghost_ref[jnp.maximum(source - row_blocks, 0)]
        operand = jnp.where(source < row_blocks, local, ghost)
        acc_ref[row] += jnp.dot(operand, tiles_ref[g], preferred_element_type=jnp.float32)
        return carry

    lax.fori_loop(0, tiles_ref.shape[0], body, 0, unroll=8)
    center = scalar_ref[0]
    half_width = scalar_ref[1]
    if first:
        state_ref, wanted_ref, out_ref, blocks_ref, outgoing_ref = refs[:5]
        for row in range(row_blocks):
            lanes = slice(row * block_size, (row + 1) * block_size)
            term = (acc_ref[row] - center * state_ref[:, lanes]) / half_width
            out_ref[:, lanes] = term
            blocks_ref[row] = term.astype(blocks_ref.dtype)
        width = outgoing_ref.shape[1]

        def send(e, carry):
            wanted = wanted_ref[e]
            block = blocks_ref[jnp.clip(wanted, 0, row_blocks - 1)]
            outgoing_ref[e // width, e % width] = jnp.where(wanted >= 0, block, jnp.zeros_like(block))
            return carry

        lax.fori_loop(0, wanted_ref.shape[0], send, 0, unroll=8)
    else:
        first_ref, state_ref, out_ref = refs[0], refs[1], refs[2]
        for row in range(row_blocks):
            lanes = slice(row * block_size, (row + 1) * block_size)
            out_ref[:, lanes] = (
                2.0 * (acc_ref[row] - center * first_ref[:, lanes]) / half_width
                - state_ref[:, lanes]
            )


def apply_tiles(pattern_flat, scalars, tiles, local_blocks, ghost_blocks, fields, width, first=True):
    row_blocks, vec_count, block_size = local_blocks.shape
    slots = tiles.shape[0]
    field = jax.ShapeDtypeStruct((vec_count, row_blocks * block_size), jnp.float32)
    vmem = pl.BlockSpec(memory_space=pltpu.VMEM)
    smem = pl.BlockSpec(memory_space=pltpu.SMEM)
    if first:
        peers = fields[1].shape[0] // width
        out_shape = (
            field,
            jax.ShapeDtypeStruct(local_blocks.shape, jnp.bfloat16),
            jax.ShapeDtypeStruct((peers, width, vec_count, block_size), jnp.bfloat16),
        )
        field_specs = [vmem, smem]
    else:
        out_shape = field
        field_specs = [vmem, vmem]
    return pl.pallas_call(
        functools.partial(product_kernel, first),
        out_shape=out_shape,
        in_specs=[smem, smem, vmem, vmem, vmem] + field_specs,
        out_specs=(vmem, vmem, vmem) if first else vmem,
        scratch_shapes=[pltpu.VMEM((row_blocks, vec_count, block_size), jnp.float32)],
        compiler_params=pltpu.CompilerParams(vmem_limit_bytes=16 * 1024 * 1024),
        cost_estimate=pl.CostEstimate(
            flops=2 * slots * vec_count * block_size * block_size,
            transcendentals=0,
            bytes_accessed=tiles.size * 2 + ghost_blocks.size * 2 + 3 * field.size * 4,
        ),
    )(pattern_flat, scalars, tiles, local_blocks, ghost_blocks, *fields)


def assemble_kernel(slot_ref, arrived_ref, out_ref, acc_ref):
    acc_ref[...] = jnp.zeros_like(acc_ref)

    def body(p, carry):
        slot = slot_ref[p]

        @pl.when(slot >= 0)
        def _():
            acc_ref[slot] += arrived_ref[p].astype(jnp.float32)

        return carry

    lax.fori_loop(0, arrived_ref.shape[0], body, 0, unroll=8)
    out_ref[...] = acc_ref[...].astype(out_ref.dtype)


def assemble_tiles(slots, arrived, slot_count):
    peers, block_size = arrived.shape[0], arrived.shape[1]
    return pl.pallas_call(
        assemble_kernel,
        out_shape=jax.ShapeDtypeStruct((slot_count, block_size, block_size), jnp.bfloat16),
        in_specs=[pl.BlockSpec(memory_space=pltpu.SMEM), pl.BlockSpec(memory_space=pltpu.VMEM)],
        out_specs=pl.BlockSpec(memory_space=pltpu.VMEM),
        scratch_shapes=[pltpu.VMEM((slot_count, block_size, block_size), jnp.float32)],
        compiler_params=pltpu.CompilerParams(vmem_limit_bytes=8 * 1024 * 1024),
        cost_estimate=pl.CostEstimate(
            flops=arrived.size, transcendentals=0, bytes_accessed=arrived.size * 2
        ),
    )(slots, arrived)


def on_device(
    basis_values, potential, contrib_index, pattern, ghost_list, state, damp_lower, damp_upper
):
    n_rows = lax.axis_size("rows")
    n_cols = lax.axis_size("cols")
    basis_blocks, points, block_size = basis_values.shape
    vec_count = state.shape[0]
    row_blocks = state.shape[1] // block_size
    group_slots = pattern.shape[1]
    slot_count = group_slots // n_cols
    ghost_width = ghost_list.shape[2]

    ghost_ids = ghost_list[0]
    owners = jnp.arange(n_rows, dtype=jnp.int32)[:, None] * row_blocks
    requested = jnp.where(ghost_ids >= 0, ghost_ids - owners, -1)
    target_row = contrib_index[:, 0]
    to_target = target_row[:, None] == jnp.arange(n_rows, dtype=jnp.int32)[None, :]
    slot_for_target = jnp.max(jnp.where(to_target, contrib_index[:, 1:2], -1), axis=0)
    index_send = jnp.concatenate([requested, slot_for_target[:, None]], axis=1)
    index_recv = lax.all_to_all(index_send, "rows", split_axis=0, concat_axis=0, tiled=True)
    wanted_by = index_recv[:, :ghost_width]
    arrived_slots = index_recv[:, ghost_width]

    center = (damp_upper[0] + damp_lower[0]) / 2.0
    half_width = (damp_upper[0] - damp_lower[0]) / 2.0

    def own_blocks(vectors):
        return (
            vectors.astype(jnp.bfloat16)
            .reshape(vec_count, row_blocks, block_size)
            .transpose(1, 0, 2)
        )

    def ghost_payload(blocks):
        return jnp.where(
            (wanted_by >= 0)[:, :, None, None],
            blocks[jnp.clip(wanted_by, 0, row_blocks - 1)],
            jnp.zeros((), jnp.bfloat16),
        )

    def exchange_ghosts(outgoing):
        arrived = lax.all_to_all(outgoing, "rows", split_axis=0, concat_axis=0, tiled=True)
        return arrived.reshape(n_rows * ghost_width, vec_count, block_size)

    state_blocks = own_blocks(state)
    state_outgoing = ghost_payload(state_blocks)

    send_tiles = presum_tiles(contrib_index.reshape(-1), basis_values, potential, n_rows)
    arrived_tiles = lax.all_to_all(send_tiles, "rows", split_axis=0, concat_axis=0, tiled=True)
    arrived_tiles, state_outgoing = lax.optimization_barrier((arrived_tiles, state_outgoing))
    state_ghosts = exchange_ghosts(state_outgoing)
    assembled = assemble_tiles(arrived_slots, arrived_tiles, slot_count)
    group_tiles = lax.all_gather(assembled, "cols", axis=0, tiled=True)

    pattern_flat = pattern.reshape(-1)
    scalars = jnp.stack([center, half_width])
    first_term, first_blocks, first_outgoing = apply_tiles(
        pattern_flat, scalars, group_tiles, state_blocks, state_ghosts, (state, wanted_by.reshape(-1)), ghost_width
    )
    second_term = apply_tiles(
        pattern_flat,
        scalars,
        group_tiles,
        first_blocks,
        exchange_ghosts(first_outgoing),
        (first_term, state),
        ghost_width,
        first=False,
    )
    return (first_term, second_term)


def solution(mesh):
    in_specs = (
        P(("rows", "cols"), None, None),
        P(("rows", "cols")),
        P(("rows", "cols"), None),
        P("rows", None, None),
        P("rows", None, None),
        P("cols", "rows"),
        P(),
        P(),
    )
    out_specs = (P("cols", "rows"), P("cols", "rows"))
    return jax.shard_map(
        on_device, mesh=mesh, in_specs=in_specs, out_specs=out_specs, check_vma=False
    )
```

```python
import functools

import jax
import jax.numpy as jnp
from jax import lax
from jax.experimental import pallas as pl
from jax.experimental.pallas import tpu as pltpu
from jax.sharding import PartitionSpec as P

SLOTS_PER_SHARE = 16
LOCAL_SLOTS = 4


def presum_kernel(index_ref, potential_ref, basis_ref, out_ref, stacked_ref, tiles_ref, acc_ref):
    blocks, block_size = basis_ref.shape[0], basis_ref.shape[2]
    for right in range(blocks):
        weighted = basis_ref[right].astype(jnp.float32).T * potential_ref[...]
        stacked_ref[right * block_size : (right + 1) * block_size] = weighted.astype(jnp.bfloat16)
    for left in range(blocks):
        product = jnp.dot(stacked_ref[...], basis_ref[left], preferred_element_type=jnp.float32)
        for right in range(blocks):
            tiles_ref[left, right] = product[right * block_size : (right + 1) * block_size].astype(
                jnp.bfloat16
            )
    acc_ref[...] = jnp.zeros_like(acc_ref)

    def body(s, carry):
        target = index_ref[4 * s]
        acc_ref[target] += tiles_ref[index_ref[4 * s + 2], index_ref[4 * s + 3]].astype(jnp.float32)
        return carry

    lax.fori_loop(0, index_ref.shape[0] // 4, body, 0, unroll=8)
    out_ref[...] = acc_ref[...].astype(out_ref.dtype)


def presum_tiles(index_flat, basis, potential, n_rows):
    blocks, points, block_size = basis.shape
    return pl.pallas_call(
        presum_kernel,
        out_shape=jax.ShapeDtypeStruct((n_rows, block_size, block_size), jnp.bfloat16),
        in_specs=[
            pl.BlockSpec(memory_space=pltpu.SMEM),
            pl.BlockSpec(memory_space=pltpu.VMEM),
            pl.BlockSpec(memory_space=pltpu.VMEM),
        ],
        out_specs=pl.BlockSpec(memory_space=pltpu.VMEM),
        scratch_shapes=[
            pltpu.VMEM((blocks * block_size, points), jnp.bfloat16),
            pltpu.VMEM((blocks, blocks, block_size, block_size), jnp.bfloat16),
            pltpu.VMEM((n_rows, block_size, block_size), jnp.float32),
        ],
        compiler_params=pltpu.CompilerParams(vmem_limit_bytes=24 * 1024 * 1024),
        cost_estimate=pl.CostEstimate(
            flops=2 * blocks * blocks * points * block_size * block_size,
            transcendentals=0,
            bytes_accessed=2 * basis.size * 2 + n_rows * block_size * block_size * 2,
        ),
    )(index_flat, potential[None, :], basis)


def product_kernel(first, pattern_ref, scalar_ref, tiles_ref, local_ref, ghost_ref, *refs):
    row_blocks, vec_count, block_size = local_ref.shape
    acc_ref = refs[-1]
    acc_ref[...] = jnp.zeros_like(acc_ref)

    ghost_count = ghost_ref.shape[0]

    def body(share, carry):
        for j in range(SLOTS_PER_SHARE):
            g = share * SLOTS_PER_SHARE + j
            row = pattern_ref[2 * g]
            source = pattern_ref[2 * g + 1]
            if j < LOCAL_SLOTS:
                operand = local_ref[jnp.clip(source, 0, row_blocks - 1)]
            else:
                operand = ghost_ref[jnp.clip(source - row_blocks, 0, ghost_count - 1)]
            acc_ref[row] += jnp.dot(operand, tiles_ref[g], preferred_element_type=jnp.float32)
        return carry

    lax.fori_loop(0, tiles_ref.shape[0] // SLOTS_PER_SHARE, body, 0)
    center = scalar_ref[0]
    half_width = scalar_ref[1]
    if first:
        state_ref, wanted_ref, out_ref, blocks_ref, outgoing_ref = refs[:5]
        for row in range(row_blocks):
            lanes = slice(row * block_size, (row + 1) * block_size)
            term = (acc_ref[row] - center * state_ref[:, lanes]) / half_width
            out_ref[:, lanes] = term
            blocks_ref[row] = term.astype(blocks_ref.dtype)
        width = outgoing_ref.shape[1]

        def send(e, carry):
            wanted = wanted_ref[e]
            block = blocks_ref[jnp.clip(wanted, 0, row_blocks - 1)]
            outgoing_ref[e // width, e % width] = jnp.where(wanted >= 0, block, jnp.zeros_like(block))
            return carry

        lax.fori_loop(0, wanted_ref.shape[0], send, 0, unroll=8)
    else:
        first_ref, state_ref, out_ref = refs[0], refs[1], refs[2]
        for row in range(row_blocks):
            lanes = slice(row * block_size, (row + 1) * block_size)
            out_ref[:, lanes] = (
                2.0 * (acc_ref[row] - center * first_ref[:, lanes]) / half_width
                - state_ref[:, lanes]
            )


def apply_tiles(pattern_flat, scalars, tiles, local_blocks, ghost_blocks, fields, width, first=True):
    row_blocks, vec_count, block_size = local_blocks.shape
    slots = tiles.shape[0]
    field = jax.ShapeDtypeStruct((vec_count, row_blocks * block_size), jnp.float32)
    vmem = pl.BlockSpec(memory_space=pltpu.VMEM)
    smem = pl.BlockSpec(memory_space=pltpu.SMEM)
    if first:
        peers = fields[1].shape[0] // width
        out_shape = (
            field,
            jax.ShapeDtypeStruct(local_blocks.shape, jnp.bfloat16),
            jax.ShapeDtypeStruct((peers, width, vec_count, block_size), jnp.bfloat16),
        )
        field_specs = [vmem, smem]
    else:
        out_shape = field
        field_specs = [vmem, vmem]
    return pl.pallas_call(
        functools.partial(product_kernel, first),
        out_shape=out_shape,
        in_specs=[smem, smem, vmem, vmem, vmem] + field_specs,
        out_specs=(vmem, vmem, vmem) if first else vmem,
        scratch_shapes=[pltpu.VMEM((row_blocks, vec_count, block_size), jnp.float32)],
        compiler_params=pltpu.CompilerParams(vmem_limit_bytes=16 * 1024 * 1024),
        cost_estimate=pl.CostEstimate(
            flops=2 * slots * vec_count * block_size * block_size,
            transcendentals=0,
            bytes_accessed=tiles.size * 2 + ghost_blocks.size * 2 + 3 * field.size * 4,
        ),
    )(pattern_flat, scalars, tiles, local_blocks, ghost_blocks, *fields)


def on_device(
    basis_values, potential, contrib_index, pattern, ghost_list, state, damp_lower, damp_upper
):
    n_rows = lax.axis_size("rows")
    n_cols = lax.axis_size("cols")
    basis_blocks, points, block_size = basis_values.shape
    vec_count = state.shape[0]
    row_blocks = state.shape[1] // block_size
    group_slots = pattern.shape[1]
    slot_count = group_slots // n_cols
    ghost_width = ghost_list.shape[2]

    ghost_ids = ghost_list[0]
    owners = jnp.arange(n_rows, dtype=jnp.int32)[:, None] * row_blocks
    requested = jnp.where(ghost_ids >= 0, ghost_ids - owners, -1)
    target_row = contrib_index[:, 0]
    to_target = target_row[:, None] == jnp.arange(n_rows, dtype=jnp.int32)[None, :]
    slot_for_target = jnp.max(jnp.where(to_target, contrib_index[:, 1:2], -1), axis=0)
    index_send = jnp.concatenate([requested, slot_for_target[:, None]], axis=1)
    index_recv = lax.all_to_all(index_send, "rows", split_axis=0, concat_axis=0, tiled=True)
    wanted_by = index_recv[:, :ghost_width]
    arrived_slots = index_recv[:, ghost_width]

    center = (damp_upper[0] + damp_lower[0]) / 2.0
    half_width = (damp_upper[0] - damp_lower[0]) / 2.0

    def own_blocks(vectors):
        return (
            vectors.astype(jnp.bfloat16)
            .reshape(vec_count, row_blocks, block_size)
            .transpose(1, 0, 2)
        )

    def ghost_payload(blocks):
        return jnp.where(
            (wanted_by >= 0)[:, :, None, None],
            blocks[jnp.clip(wanted_by, 0, row_blocks - 1)],
            jnp.zeros((), jnp.bfloat16),
        )

    def exchange_ghosts(outgoing):
        arrived = lax.all_to_all(outgoing, "rows", split_axis=0, concat_axis=0, tiled=True)
        return arrived.reshape(n_rows * ghost_width, vec_count, block_size)

    state_blocks = own_blocks(state)
    state_outgoing = ghost_payload(state_blocks)

    send_tiles = presum_tiles(contrib_index.reshape(-1), basis_values, potential, n_rows)
    arrived_tiles = lax.all_to_all(send_tiles, "rows", split_axis=0, concat_axis=0, tiled=True)
    arrived_tiles, state_outgoing = lax.optimization_barrier((arrived_tiles, state_outgoing))
    state_ghosts = exchange_ghosts(state_outgoing)
    slot_wanted = jnp.arange(slot_count, dtype=jnp.int32)
    selector = (arrived_slots[None, :] == slot_wanted[:, None]).astype(jnp.bfloat16)
    assembled = jnp.dot(
        selector,
        arrived_tiles.reshape(n_rows, block_size * block_size),
        preferred_element_type=jnp.float32,
    )
    assembled = assembled.astype(jnp.bfloat16).reshape(slot_count, block_size, block_size)
    group_tiles = lax.all_gather(assembled, "cols", axis=0, tiled=True)

    pattern_flat = pattern.reshape(-1)
    scalars = jnp.stack([center, half_width])
    first_term, first_blocks, first_outgoing = apply_tiles(
        pattern_flat, scalars, group_tiles, state_blocks, state_ghosts, (state, wanted_by.reshape(-1)), ghost_width
    )
    second_term = apply_tiles(
        pattern_flat,
        scalars,
        group_tiles,
        first_blocks,
        exchange_ghosts(first_outgoing),
        (first_term, state),
        ghost_width,
        first=False,
    )
    return (first_term, second_term)


def solution(mesh):
    in_specs = (
        P(("rows", "cols"), None, None),
        P(("rows", "cols")),
        P(("rows", "cols"), None),
        P("rows", None, None),
        P("rows", None, None),
        P("cols", "rows"),
        P(),
        P(),
    )
    out_specs = (P("cols", "rows"), P("cols", "rows"))
    return jax.shard_map(
        on_device, mesh=mesh, in_specs=in_specs, out_specs=out_specs, check_vma=False
    )
```

```python
import functools

import jax
import jax.numpy as jnp
from jax import lax
from jax.experimental import pallas as pl
from jax.experimental.pallas import tpu as pltpu
from jax.sharding import PartitionSpec as P

SLOTS_PER_SHARE = 16
LOCAL_SLOTS = 4


def presum_kernel(index_ref, potential_ref, basis_ref, out_ref, stacked_ref, tiles_ref, acc_ref):
    blocks, block_size = basis_ref.shape[0], basis_ref.shape[2]
    for right in range(blocks):
        weighted = basis_ref[right].astype(jnp.float32).T * potential_ref[...]
        stacked_ref[right * block_size : (right + 1) * block_size] = weighted.astype(jnp.bfloat16)
    for left in range(blocks):
        product = jnp.dot(stacked_ref[...], basis_ref[left], preferred_element_type=jnp.float32)
        for right in range(blocks):
            tiles_ref[left, right] = product[right * block_size : (right + 1) * block_size].astype(
                jnp.bfloat16
            )
    acc_ref[...] = jnp.zeros_like(acc_ref)

    def body(s, carry):
        target = index_ref[4 * s]
        acc_ref[target] += tiles_ref[index_ref[4 * s + 2], index_ref[4 * s + 3]].astype(jnp.float32)
        return carry

    lax.fori_loop(0, index_ref.shape[0] // 4, body, 0, unroll=8)
    out_ref[...] = acc_ref[...].astype(out_ref.dtype)


def presum_tiles(index_flat, basis, potential, n_rows):
    blocks, points, block_size = basis.shape
    return pl.pallas_call(
        presum_kernel,
        out_shape=jax.ShapeDtypeStruct((n_rows, block_size, block_size), jnp.bfloat16),
        in_specs=[
            pl.BlockSpec(memory_space=pltpu.SMEM),
            pl.BlockSpec(memory_space=pltpu.VMEM),
            pl.BlockSpec(memory_space=pltpu.VMEM),
        ],
        out_specs=pl.BlockSpec(memory_space=pltpu.VMEM),
        scratch_shapes=[
            pltpu.VMEM((blocks * block_size, points), jnp.bfloat16),
            pltpu.VMEM((blocks, blocks, block_size, block_size), jnp.bfloat16),
            pltpu.VMEM((n_rows, block_size, block_size), jnp.float32),
        ],
        compiler_params=pltpu.CompilerParams(vmem_limit_bytes=24 * 1024 * 1024),
        cost_estimate=pl.CostEstimate(
            flops=2 * blocks * blocks * points * block_size * block_size,
            transcendentals=0,
            bytes_accessed=2 * basis.size * 2 + n_rows * block_size * block_size * 2,
        ),
    )(index_flat, potential[None, :], basis)


def product_kernel(first, pattern_ref, scalar_ref, tiles_ref, local_ref, ghost_ref, *refs):
    row_blocks, vec_count, block_size = local_ref.shape
    acc_ref = refs[-1]
    acc_ref[...] = jnp.zeros_like(acc_ref)

    ghost_count = ghost_ref.shape[0]

    def body(share, carry):
        for j in range(SLOTS_PER_SHARE):
            g = share * SLOTS_PER_SHARE + j
            row = pattern_ref[2 * g]
            source = pattern_ref[2 * g + 1]
            if j < LOCAL_SLOTS:
                operand = local_ref[jnp.clip(source, 0, row_blocks - 1)]
            else:
                operand = ghost_ref[jnp.clip(source - row_blocks, 0, ghost_count - 1)]
            acc_ref[row] += jnp.dot(operand, tiles_ref[g], preferred_element_type=jnp.float32)
        return carry

    lax.fori_loop(0, tiles_ref.shape[0] // SLOTS_PER_SHARE, body, 0)
    center = scalar_ref[0]
    half_width = scalar_ref[1]
    if first:
        state_ref, wanted_ref, out_ref, blocks_ref, outgoing_ref = refs[:5]
        for row in range(row_blocks):
            lanes = slice(row * block_size, (row + 1) * block_size)
            term = (acc_ref[row] - center * state_ref[:, lanes]) / half_width
            out_ref[:, lanes] = term
            blocks_ref[row] = term.astype(blocks_ref.dtype)
        width = outgoing_ref.shape[1]

        def send(e, carry):
            outgoing_ref[e // width, e % width] = blocks_ref[jnp.clip(wanted_ref[e], 0, row_blocks - 1)]
            return carry

        lax.fori_loop(0, wanted_ref.shape[0], send, 0, unroll=8)
    else:
        first_ref, state_ref, out_ref = refs[0], refs[1], refs[2]
        for row in range(row_blocks):
            lanes = slice(row * block_size, (row + 1) * block_size)
            out_ref[:, lanes] = (
                2.0 * (acc_ref[row] - center * first_ref[:, lanes]) / half_width
                - state_ref[:, lanes]
            )


def apply_tiles(pattern_flat, scalars, tiles, local_blocks, ghost_blocks, fields, width, first=True):
    row_blocks, vec_count, block_size = local_blocks.shape
    slots = tiles.shape[0]
    field = jax.ShapeDtypeStruct((vec_count, row_blocks * block_size), jnp.float32)
    vmem = pl.BlockSpec(memory_space=pltpu.VMEM)
    smem = pl.BlockSpec(memory_space=pltpu.SMEM)
    if first:
        peers = fields[1].shape[0] // width
        out_shape = (
            field,
            jax.ShapeDtypeStruct(local_blocks.shape, jnp.bfloat16),
            jax.ShapeDtypeStruct((peers, width, vec_count, block_size), jnp.bfloat16),
        )
        field_specs = [vmem, smem]
    else:
        out_shape = field
        field_specs = [vmem, vmem]
    return pl.pallas_call(
        functools.partial(product_kernel, first),
        out_shape=out_shape,
        in_specs=[smem, smem, vmem, vmem, vmem] + field_specs,
        out_specs=(vmem, vmem, vmem) if first else vmem,
        scratch_shapes=[pltpu.VMEM((row_blocks, vec_count, block_size), jnp.float32)],
        compiler_params=pltpu.CompilerParams(vmem_limit_bytes=16 * 1024 * 1024),
        cost_estimate=pl.CostEstimate(
            flops=2 * slots * vec_count * block_size * block_size,
            transcendentals=0,
            bytes_accessed=tiles.size * 2 + ghost_blocks.size * 2 + 3 * field.size * 4,
        ),
    )(pattern_flat, scalars, tiles, local_blocks, ghost_blocks, *fields)


def on_device(
    basis_values, potential, contrib_index, pattern, ghost_list, state, damp_lower, damp_upper
):
    n_rows = lax.axis_size("rows")
    n_cols = lax.axis_size("cols")
    basis_blocks, points, block_size = basis_values.shape
    vec_count = state.shape[0]
    row_blocks = state.shape[1] // block_size
    group_slots = pattern.shape[1]
    slot_count = group_slots // n_cols
    ghost_width = ghost_list.shape[2]

    ghost_ids = ghost_list[0]
    owners = jnp.arange(n_rows, dtype=jnp.int32)[:, None] * row_blocks
    requested = jnp.where(ghost_ids >= 0, ghost_ids - owners, -1)
    target_row = contrib_index[:, 0]
    to_target = target_row[:, None] == jnp.arange(n_rows, dtype=jnp.int32)[None, :]
    slot_for_target = jnp.max(jnp.where(to_target, contrib_index[:, 1:2], -1), axis=0)
    index_send = jnp.concatenate([requested, slot_for_target[:, None]], axis=1)
    index_recv = lax.all_to_all(index_send, "rows", split_axis=0, concat_axis=0, tiled=True)
    wanted_by = index_recv[:, :ghost_width]
    arrived_slots = index_recv[:, ghost_width]

    center = (damp_upper[0] + damp_lower[0]) / 2.0
    half_width = (damp_upper[0] - damp_lower[0]) / 2.0

    def own_blocks(vectors):
        return (
            vectors.astype(jnp.bfloat16)
            .reshape(vec_count, row_blocks, block_size)
            .transpose(1, 0, 2)
        )

    def ghost_payload(blocks):
        return jnp.where(
            (wanted_by >= 0)[:, :, None, None],
            blocks[jnp.clip(wanted_by, 0, row_blocks - 1)],
            jnp.zeros((), jnp.bfloat16),
        )

    def exchange_ghosts(outgoing):
        arrived = lax.all_to_all(outgoing, "rows", split_axis=0, concat_axis=0, tiled=True)
        return arrived.reshape(n_rows * ghost_width, vec_count, block_size)

    state_blocks = own_blocks(state)
    state_outgoing = ghost_payload(state_blocks)

    send_tiles = presum_tiles(contrib_index.reshape(-1), basis_values, potential, n_rows)
    arrived_tiles = lax.all_to_all(send_tiles, "rows", split_axis=0, concat_axis=0, tiled=True)
    arrived_tiles, state_outgoing = lax.optimization_barrier((arrived_tiles, state_outgoing))
    state_ghosts = exchange_ghosts(state_outgoing)
    slot_wanted = jnp.arange(slot_count, dtype=jnp.int32)
    selector = (arrived_slots[None, :] == slot_wanted[:, None]).astype(jnp.bfloat16)
    assembled = jnp.dot(
        selector,
        arrived_tiles.reshape(n_rows, block_size * block_size),
        preferred_element_type=jnp.float32,
    )
    assembled = assembled.astype(jnp.bfloat16).reshape(slot_count, block_size, block_size)
    group_tiles = lax.all_gather(assembled, "cols", axis=0, tiled=True)

    pattern_flat = pattern.reshape(-1)
    scalars = jnp.stack([center, half_width])
    first_term, first_blocks, first_outgoing = apply_tiles(
        pattern_flat, scalars, group_tiles, state_blocks, state_ghosts, (state, wanted_by.reshape(-1)), ghost_width
    )
    second_term = apply_tiles(
        pattern_flat,
        scalars,
        group_tiles,
        first_blocks,
        exchange_ghosts(first_outgoing),
        (first_term, state),
        ghost_width,
        first=False,
    )
    return (first_term, second_term)


def solution(mesh):
    in_specs = (
        P(("rows", "cols"), None, None),
        P(("rows", "cols")),
        P(("rows", "cols"), None),
        P("rows", None, None),
        P("rows", None, None),
        P("cols", "rows"),
        P(),
        P(),
    )
    out_specs = (P("cols", "rows"), P("cols", "rows"))
    return jax.shard_map(
        on_device, mesh=mesh, in_specs=in_specs, out_specs=out_specs, check_vma=False
    )
```

```python
import functools

import jax
import jax.numpy as jnp
from jax import lax
from jax.experimental import pallas as pl
from jax.experimental.pallas import tpu as pltpu
from jax.sharding import PartitionSpec as P

SLOTS_PER_SHARE = 16
LOCAL_SLOTS = 4


def presum_kernel(index_ref, potential_ref, basis_ref, out_ref, stacked_ref, tiles_ref, acc_ref):
    blocks, block_size = basis_ref.shape[0], basis_ref.shape[2]
    for right in range(blocks):
        weighted = basis_ref[right].astype(jnp.float32).T * potential_ref[...]
        stacked_ref[right * block_size : (right + 1) * block_size] = weighted.astype(jnp.bfloat16)
    for left in range(blocks):
        product = jnp.dot(stacked_ref[...], basis_ref[left], preferred_element_type=jnp.float32)
        for right in range(blocks):
            tiles_ref[left, right] = product[right * block_size : (right + 1) * block_size].astype(
                jnp.bfloat16
            )
    acc_ref[...] = jnp.zeros_like(acc_ref)

    def body(s, carry):
        target = index_ref[4 * s]
        acc_ref[target] += tiles_ref[index_ref[4 * s + 2], index_ref[4 * s + 3]].astype(jnp.float32)
        return carry

    lax.fori_loop(0, index_ref.shape[0] // 4, body, 0, unroll=16)
    out_ref[...] = acc_ref[...].astype(out_ref.dtype)


def presum_tiles(index_flat, basis, potential, n_rows):
    blocks, points, block_size = basis.shape
    return pl.pallas_call(
        presum_kernel,
        out_shape=jax.ShapeDtypeStruct((n_rows, block_size, block_size), jnp.bfloat16),
        in_specs=[
            pl.BlockSpec(memory_space=pltpu.SMEM),
            pl.BlockSpec(memory_space=pltpu.VMEM),
            pl.BlockSpec(memory_space=pltpu.VMEM),
        ],
        out_specs=pl.BlockSpec(memory_space=pltpu.VMEM),
        scratch_shapes=[
            pltpu.VMEM((blocks * block_size, points), jnp.bfloat16),
            pltpu.VMEM((blocks, blocks, block_size, block_size), jnp.bfloat16),
            pltpu.VMEM((n_rows, block_size, block_size), jnp.float32),
        ],
        compiler_params=pltpu.CompilerParams(vmem_limit_bytes=24 * 1024 * 1024),
        cost_estimate=pl.CostEstimate(
            flops=2 * blocks * blocks * points * block_size * block_size,
            transcendentals=0,
            bytes_accessed=2 * basis.size * 2 + n_rows * block_size * block_size * 2,
        ),
    )(index_flat, potential[None, :], basis)


def product_kernel(first, pattern_ref, scalar_ref, tiles_ref, local_ref, ghost_ref, *refs):
    row_blocks, vec_count, block_size = local_ref.shape
    acc_ref = refs[-1]
    acc_ref[...] = jnp.zeros_like(acc_ref)

    ghost_count = ghost_ref.shape[0]

    def body(share, carry):
        for j in range(SLOTS_PER_SHARE):
            g = share * SLOTS_PER_SHARE + j
            row = pattern_ref[2 * g]
            source = pattern_ref[2 * g + 1]
            if j < LOCAL_SLOTS:
                operand = local_ref[jnp.clip(source, 0, row_blocks - 1)]
            else:
                operand = ghost_ref[jnp.clip(source - row_blocks, 0, ghost_count - 1)]
            acc_ref[row] += jnp.dot(operand, tiles_ref[g], preferred_element_type=jnp.float32)
        return carry

    lax.fori_loop(0, tiles_ref.shape[0] // SLOTS_PER_SHARE, body, 0)
    center = scalar_ref[0]
    half_width = scalar_ref[1]
    if first:
        state_ref, wanted_ref, out_ref, blocks_ref, outgoing_ref = refs[:5]
        for row in range(row_blocks):
            lanes = slice(row * block_size, (row + 1) * block_size)
            term = (acc_ref[row] - center * state_ref[:, lanes]) / half_width
            out_ref[:, lanes] = term
            blocks_ref[row] = term.astype(blocks_ref.dtype)
        width = outgoing_ref.shape[1]

        def send(e, carry):
            wanted = wanted_ref[e]
            block = blocks_ref[jnp.clip(wanted, 0, row_blocks - 1)]
            outgoing_ref[e // width, e % width] = jnp.where(wanted >= 0, block, jnp.zeros_like(block))
            return carry

        lax.fori_loop(0, wanted_ref.shape[0], send, 0, unroll=8)
    else:
        first_ref, state_ref, out_ref = refs[0], refs[1], refs[2]
        for row in range(row_blocks):
            lanes = slice(row * block_size, (row + 1) * block_size)
            out_ref[:, lanes] = (
                2.0 * (acc_ref[row] - center * first_ref[:, lanes]) / half_width
                - state_ref[:, lanes]
            )


def apply_tiles(pattern_flat, scalars, tiles, local_blocks, ghost_blocks, fields, width, first=True):
    row_blocks, vec_count, block_size = local_blocks.shape
    slots = tiles.shape[0]
    field = jax.ShapeDtypeStruct((vec_count, row_blocks * block_size), jnp.float32)
    vmem = pl.BlockSpec(memory_space=pltpu.VMEM)
    smem = pl.BlockSpec(memory_space=pltpu.SMEM)
    if first:
        peers = fields[1].shape[0] // width
        out_shape = (
            field,
            jax.ShapeDtypeStruct(local_blocks.shape, jnp.bfloat16),
            jax.ShapeDtypeStruct((peers, width, vec_count, block_size), jnp.bfloat16),
        )
        field_specs = [vmem, smem]
    else:
        out_shape = field
        field_specs = [vmem, vmem]
    return pl.pallas_call(
        functools.partial(product_kernel, first),
        out_shape=out_shape,
        in_specs=[smem, smem, vmem, vmem, vmem] + field_specs,
        out_specs=(vmem, vmem, vmem) if first else vmem,
        scratch_shapes=[pltpu.VMEM((row_blocks, vec_count, block_size), jnp.float32)],
        compiler_params=pltpu.CompilerParams(vmem_limit_bytes=16 * 1024 * 1024),
        cost_estimate=pl.CostEstimate(
            flops=2 * slots * vec_count * block_size * block_size,
            transcendentals=0,
            bytes_accessed=tiles.size * 2 + ghost_blocks.size * 2 + 3 * field.size * 4,
        ),
    )(pattern_flat, scalars, tiles, local_blocks, ghost_blocks, *fields)


def on_device(
    basis_values, potential, contrib_index, pattern, ghost_list, state, damp_lower, damp_upper
):
    n_rows = lax.axis_size("rows")
    n_cols = lax.axis_size("cols")
    basis_blocks, points, block_size = basis_values.shape
    vec_count = state.shape[0]
    row_blocks = state.shape[1] // block_size
    group_slots = pattern.shape[1]
    slot_count = group_slots // n_cols
    ghost_width = ghost_list.shape[2]

    ghost_ids = ghost_list[0]
    owners = jnp.arange(n_rows, dtype=jnp.int32)[:, None] * row_blocks
    requested = jnp.where(ghost_ids >= 0, ghost_ids - owners, -1)
    target_row = contrib_index[:, 0]
    to_target = target_row[:, None] == jnp.arange(n_rows, dtype=jnp.int32)[None, :]
    slot_for_target = jnp.max(jnp.where(to_target, contrib_index[:, 1:2], -1), axis=0)
    index_send = jnp.concatenate([requested, slot_for_target[:, None]], axis=1)
    index_recv = lax.all_to_all(index_send, "rows", split_axis=0, concat_axis=0, tiled=True)
    wanted_by = index_recv[:, :ghost_width]
    arrived_slots = index_recv[:, ghost_width]

    center = (damp_upper[0] + damp_lower[0]) / 2.0
    half_width = (damp_upper[0] - damp_lower[0]) / 2.0

    def own_blocks(vectors):
        return (
            vectors.astype(jnp.bfloat16)
            .reshape(vec_count, row_blocks, block_size)
            .transpose(1, 0, 2)
        )

    def ghost_payload(blocks):
        return jnp.where(
            (wanted_by >= 0)[:, :, None, None],
            blocks[jnp.clip(wanted_by, 0, row_blocks - 1)],
            jnp.zeros((), jnp.bfloat16),
        )

    def exchange_ghosts(outgoing):
        arrived = lax.all_to_all(outgoing, "rows", split_axis=0, concat_axis=0, tiled=True)
        return arrived.reshape(n_rows * ghost_width, vec_count, block_size)

    state_blocks = own_blocks(state)
    state_outgoing = ghost_payload(state_blocks)

    send_tiles = presum_tiles(contrib_index.reshape(-1), basis_values, potential, n_rows)
    arrived_tiles = lax.all_to_all(send_tiles, "rows", split_axis=0, concat_axis=0, tiled=True)
    arrived_tiles, state_outgoing = lax.optimization_barrier((arrived_tiles, state_outgoing))
    state_ghosts = exchange_ghosts(state_outgoing)
    slot_wanted = jnp.arange(slot_count, dtype=jnp.int32)
    selector = (arrived_slots[None, :] == slot_wanted[:, None]).astype(jnp.bfloat16)
    assembled = jnp.dot(
        selector,
        arrived_tiles.reshape(n_rows, block_size * block_size),
        preferred_element_type=jnp.float32,
    )
    assembled = assembled.astype(jnp.bfloat16).reshape(slot_count, block_size, block_size)
    group_tiles = lax.all_gather(assembled, "cols", axis=0, tiled=True)

    pattern_flat = pattern.reshape(-1)
    scalars = jnp.stack([center, half_width])
    first_term, first_blocks, first_outgoing = apply_tiles(
        pattern_flat, scalars, group_tiles, state_blocks, state_ghosts, (state, wanted_by.reshape(-1)), ghost_width
    )
    second_term = apply_tiles(
        pattern_flat,
        scalars,
        group_tiles,
        first_blocks,
        exchange_ghosts(first_outgoing),
        (first_term, state),
        ghost_width,
        first=False,
    )
    return (first_term, second_term)


def solution(mesh):
    in_specs = (
        P(("rows", "cols"), None, None),
        P(("rows", "cols")),
        P(("rows", "cols"), None),
        P("rows", None, None),
        P("rows", None, None),
        P("cols", "rows"),
        P(),
        P(),
    )
    out_specs = (P("cols", "rows"), P("cols", "rows"))
    return jax.shard_map(
        on_device, mesh=mesh, in_specs=in_specs, out_specs=out_specs, check_vma=False
    )
```
